32 devices in a mesh: pw: 8 (over z, core), band: 4 (over y, x).
Axes of the slice: x: 2, y: 2, z: 4, core: 2. Of those that a mesh axis runs over, the one named last changes fastest.
Arguments:
- psi_res: bfloat16 [256, 2, 72, 1024], P('band', None, None, 'pw'), may hold values from -0.015625 to 0.015625
- correction: float32 [4, 2, 72, 1024], P('band', None, None, 'pw'), may hold values from -24 to 24
- local_potential: float32 [128, 128, 128], P('pw'), may hold values from -2 to 1
- stick_xy: int32 [1024], P('pw'), may hold values from 0 to 16383, as said below
Outputs:
- residual: float32 [4, 2, 72, 1024], P('band', None, None, 'pw')
- hamiltonian_proj: float32 [2, 256, 4], P(None, 'band')
- intersection_proj: float32 [2, 256, 4], P(None, 'band')
The draws below stay inside these ranges and needn't reach their ends.
Inputs may be any that keep to these rules, and one draw needn't show every extreme that they name: `stick_xy`: distinct positions: the 1024 positions of the x-y plane nearest the anchor of the periodic grid, ties broken at random, in an order drawn from the seed.
All inputs are finite; a program needn't handle non-finite values.
Results may differ from the reference program's by a relative error of at most 0.0029.
Values may be sent and summed in bfloat16 or wider, within the bound.
No kernel may reach another device: no remote copies, remote signals or barrier semaphores. Data moves between devices by JAX's collectives and lax.ppermute only.
A program may use at most 128 MiB of HBM per device.

```python
import jax
import jax.numpy as jnp
from jax import lax

NG = 128
ZL = 72
STICKS = 1024
NRES = 256
NCOR = 4


def draw_correction(key, part):
    full_shape = (NCOR, 2, ZL, STICKS)
    stick_ramp = 0.6 + 1.2 * jnp.arange(STICKS, dtype=jnp.float32) / STICKS
    normal_part = jnp.clip(jax.random.normal(key, full_shape, jnp.float32), -5.0, 5.0)
    return normal_part * stick_ramp


def draw_stick_xy(key, part):
    key_one, key_two = jax.random.split(key)
    grid_cells = jnp.arange(NG * NG, dtype=jnp.int32)
    across = grid_cells // NG
    along = grid_cells % NG
    freq_x = jnp.where(across < NG // 2, across, across - NG)
    freq_y = jnp.where(along < NG // 2, along, along - NG)
    radius = freq_x * freq_x + freq_y * freq_y
    shuffle = jax.random.permutation(key_one, NG * NG).astype(jnp.int32)
    scores = radius * (NG * NG) + shuffle
    ranking = jnp.argsort(scores, stable=True)
    chosen = ranking[:STICKS].astype(jnp.int32)
    return chosen[jax.random.permutation(key_two, STICKS)].astype(jnp.int32)


def levels(rng, dims, pieces, low, high):
    level = 1.0
    for position, parts in pieces:
        draws = jax.random.uniform(jax.random.fold_in(jax.random.fold_in(rng, 6), position), (parts,), jnp.float32, low / len(pieces), high / len(pieces))
        level = level * jnp.repeat(jnp.exp(draws), dims[position] // parts).reshape((-1,) + (1,) * (len(dims) - 1 - position))
    return level


def gaussian(key, shape, scale, reach, cuts=(), held_as=jnp.bfloat16):
    entries = jax.random.normal(key, shape, jnp.float32) * scale
    if len(cuts) > 0:
        entries = levels(key, shape, cuts, -0.22, 0.18) * entries
    return jnp.clip(entries, min=-reach, max=reach).astype(held_as)


def setup_inputs(seed: int = 0) -> dict:
    seeds = jax.random.split(jax.random.key(seed), 5)
    psi_res = gaussian(seeds[0], (NRES, 2, ZL, STICKS), (2 * ZL * STICKS) ** -0.5, 0.015625, ((0, 4), (3, 8)))
    correction = draw_correction(jax.random.fold_in(seeds[4], 71), 0)
    local_potential = jnp.clip(-2.0 + 3.0 * jax.random.uniform(seeds[2], (NG, NG, NG), jnp.float32) ** levels(seeds[2], (NG, NG, NG), ((0, 8),), -0.2, 0.2), -2.0, 1.0)
    stick_xy = draw_stick_xy(jax.random.fold_in(seeds[4], 71), 0)
    return {"psi_res": psi_res, "correction": correction, "local_potential": local_potential, "stick_xy": stick_xy}


kinetic_unit = 0.002


def signed_freq(index, grid_size):
    return jnp.where(index < grid_size // 2, index, index - grid_size)


def reference(psi_res, correction, local_potential, stick_xy):
    stick_x = signed_freq(stick_xy // NG, NG)
    stick_y = signed_freq(stick_xy % NG, NG)
    z_freq = jnp.arange(ZL, dtype=jnp.int32) - ZL // 2
    z_index = jnp.mod(z_freq, NG).astype(jnp.int32)
    kinetic = kinetic_unit * (z_freq[:, None] ** 2 + (stick_x ** 2 + stick_y ** 2)[None, :]).astype(jnp.float32)

    def apply_one(coefs):
        values = lax.complex(coefs[0], coefs[1])
        grid_field = jnp.zeros((NG, NG * NG), dtype=values.dtype)
        grid_field = grid_field.at[z_index[:, None], stick_xy[None, :]].set(values)
        real_space = jnp.fft.ifftn(grid_field.reshape(NG, NG, NG)) * (NG ** 3)
        spectrum = jnp.fft.fftn(real_space * local_potential) / (NG ** 3)
        picked = spectrum.reshape(NG, NG * NG)[z_index][:, stick_xy]
        return jnp.stack([jnp.real(picked), jnp.imag(picked)], 0)

    applied = lax.map(apply_one, correction)
    image = kinetic * correction + applied
    numerator = jnp.sum(correction * image, axis=(1, 2, 3))
    denominator = jnp.sum(correction * correction, axis=(1, 2, 3))
    rayleigh = numerator / denominator
    residual = image - rayleigh[:, None, None, None] * correction
    rounded_corr = correction.astype(jnp.bfloat16)
    rounded_image = image.astype(jnp.bfloat16)
    length = ZL * STICKS
    psi_flat = psi_res.reshape(NRES, 2 * length)
    psi_swap = jnp.concatenate([-psi_res[:, 1].reshape(NRES, length), psi_res[:, 0].reshape(NRES, length)], 1)

    def project(vectors):
        flat_rows = vectors.reshape(NCOR, 2 * length)
        real_part = jnp.dot(psi_flat, flat_rows.T, preferred_element_type=jnp.float32)
        imag_part = jnp.dot(psi_swap, flat_rows.T, preferred_element_type=jnp.float32)
        return jnp.stack([real_part, imag_part], 0)

    return residual, project(rounded_image), project(rounded_corr)
```

```python
import math

import jax
import jax.numpy as jnp
import numpy as np
from jax import lax
from jax.experimental import pallas as pl
from jax.experimental.pallas import tpu as pltpu
from jax.sharding import PartitionSpec as P

kinetic_unit = 0.002
highest = lax.Precision.HIGHEST
lanes = 128
f32 = jnp.float32
bf16 = jnp.bfloat16


def round_up(count, step):
    return -(-count // step) * step


def signed_freq(index, grid_size):
    return jnp.where(index < grid_size // 2, index, index - grid_size)


def phases(out_index, in_index, direction, grid_size):
    angles = (out_index[:, None] * in_index[None, :]) % grid_size * (2.0 * math.pi / grid_size)
    cosine, sine = np.cos(angles), direction * np.sin(angles)
    return np.stack([np.stack([cosine, -sine], 1), np.stack([sine, cosine], 1)], 0)


def split(table, count):
    pieces = []
    rest = np.asarray(table, np.float64)
    for _ in range(count):
        piece = rest.astype(jnp.bfloat16)
        pieces.append(piece)
        rest = rest - piece.astype(np.float64)
    return pieces


class Sizes:
    def __init__(self, groups, planes, grid_size, stick_depth, sticks_local):
        self.groups, self.planes = groups, planes
        self.grid, self.depth, self.sticks_local = grid_size, stick_depth, sticks_local
        self.rows = round_up(planes, 16)
        self.sticks = groups * sticks_local
        self.box = round_up(2 * math.ceil(math.sqrt(self.sticks / math.pi)) + 2, 8)
        self.pair = 2 * self.box
        self.pair_pad = round_up(self.pair, lanes)


def z_rows(sizes):
    group = np.repeat(np.arange(sizes.groups), sizes.rows)
    plane = np.tile(np.arange(sizes.rows), sizes.groups)
    return group * sizes.planes + plane, plane < sizes.planes


def z_back_table(sizes):
    z_freq = np.arange(sizes.depth) - sizes.depth // 2
    z_index, real = z_rows(sizes)
    table = phases(z_index, z_freq, 1, sizes.grid) * real[None, :, None, None]
    table = table.reshape(2, sizes.groups, sizes.rows, 2 * sizes.depth)
    return table.transpose(1, 0, 2, 3).reshape(-1, 2 * sizes.depth).astype(np.float32)


def z_forward_table(sizes):
    z_freq = np.arange(sizes.depth) - sizes.depth // 2
    z_index, real = z_rows(sizes)
    table = phases(z_freq, z_index, -1, sizes.grid) * real / float(sizes.grid**3)
    table = table.reshape(2 * sizes.depth, 2, sizes.groups, sizes.rows)
    table = table.transpose(0, 2, 1, 3).reshape(2 * sizes.depth, -1)
    return np.concatenate(split(table, 3), 0)


def plane_tables(sizes):
    grid = np.arange(sizes.grid)
    freq = np.arange(sizes.box) - sizes.box // 2
    back = phases(grid, freq, 1, sizes.grid).reshape(2 * sizes.grid, sizes.pair)
    forward = phases(freq, grid, -1, sizes.grid).reshape(sizes.pair, 2 * sizes.grid)
    back_high, back_low = split(back, 2)
    forward_high, forward_low = split(forward, 2)
    pad = ((0, sizes.pair_pad - sizes.pair), (0, 0))
    y_back = np.concatenate([np.pad(back_high.T, pad), np.pad(back_low.T, pad)], 0)
    x_back = np.concatenate([back_high, back_low, back_high], 1)
    x_forward = np.concatenate([forward_high, forward_low], 0)
    y_forward = np.concatenate([np.pad(forward_high, pad), np.pad(forward_low, pad)], 0).T
    return y_back, x_back, x_forward, y_forward


def vmem():
    return pl.BlockSpec(memory_space=pltpu.VMEM)


def spread_sticks(sizes, vector, positions):
    def kernel(table_ref, vector_ref, position_ref, out_ref):
        columns = jnp.dot(table_ref[...], vector_ref[...], precision=highest, preferred_element_type=f32)
        block = 2 * sizes.rows
        x_pos = (position_ref[...] // sizes.grid).astype(f32)
        y_pos = (position_ref[...] % sizes.grid).astype(f32)
        row = lax.broadcasted_iota(jnp.int32, (16, sizes.sticks_local), 0)
        tail = jnp.where(row == 0, x_pos, jnp.where(row == 1, y_pos, 0.0)).astype(bf16)
        for group in range(sizes.groups):
            out_ref[group, 0:block, :] = columns[group * block : (group + 1) * block].astype(bf16)
            out_ref[group, block:, :] = tail

    return pl.pallas_call(
        kernel,
        out_shape=jax.ShapeDtypeStruct((sizes.groups, 2 * sizes.rows + 16, sizes.sticks_local), bf16),
        in_specs=[vmem()] * 3,
        out_specs=vmem(),
        name="spread_sticks",
    )(jnp.asarray(z_back_table(sizes)), vector, positions[None, :])


def anchor_of(position, grid_size):
    angle = position * (2.0 * math.pi / grid_size)
    spot = lax.broadcasted_iota(jnp.int32, (1, grid_size), 1).astype(f32)
    spot_angle = spot * (2.0 * math.pi / grid_size)

    def total(values):
        return jnp.sum(jnp.sum(values, axis=0, keepdims=True), axis=1, keepdims=True)

    score = total(jnp.cos(angle)) * jnp.cos(spot_angle) + total(jnp.sin(angle)) * jnp.sin(spot_angle)
    best = jnp.max(score, axis=1, keepdims=True)
    return jnp.min(jnp.where(score >= best, spot, float(grid_size)), axis=1, keepdims=True)


def apply_planes(sizes, received, potential):
    grid, box, pair, pair_pad, rows = sizes.grid, sizes.box, sizes.pair, sizes.pair_pad, sizes.rows
    groups, local, sticks = sizes.groups, sizes.sticks_local, sizes.sticks
    y_back, x_back, x_forward, y_forward = plane_tables(sizes)

    def kernel(in_ref, pot_ref, yb_ref, xb_ref, xf_ref, yf_ref, out_ref, left_ref, hot_ref, a_ref, b_ref):
        def relative(position):
            moved = position - anchor_of(position, grid) + float(box // 2)
            moved = jnp.where(moved < 0, moved + float(grid), moved)
            return jnp.where(moved >= float(grid), moved - float(grid), moved)

        x_rel = relative(jnp.concatenate([in_ref[g, 2 * rows : 2 * rows + 16, :].astype(f32)[0:1] for g in range(groups)], 0))
        y_rel = relative(jnp.concatenate([in_ref[g, 2 * rows : 2 * rows + 16, :].astype(f32)[1:2] for g in range(groups)], 0))

        y_row = lax.broadcasted_iota(jnp.int32, (pair_pad, local), 0).astype(f32)
        for g in range(groups):
            y_here = jnp.broadcast_to(y_rel[g : g + 1], (pair_pad, local))
            for part in range(2):
                hot = jnp.where(y_row == y_here + float(part * box), 1.0, 0.0)
                hot = jnp.where(y_row < float((part + 1) * box), hot, 0.0).astype(bf16)
                where = part * sticks + g * local
                hot_ref[0:pair_pad, where : where + local] = hot
                hot_ref[pair_pad:, where : where + local] = hot
            x_here = jnp.broadcast_to(x_rel[g : g + 1], (rows, local))
            parts = [in_ref[g, part * rows : (part + 1) * rows, :].astype(f32) for part in range(2)]
            for x in range(box):
                mask = x_here == float(x)
                for part in range(2):
                    where = part * sticks + g * local
                    left_ref[x * rows : (x + 1) * rows, where : where + local] = jnp.where(mask, parts[part], 0.0).astype(bf16)

        placed = lax.dot_general(left_ref[...], hot_ref[...], (((1,), (1,)), ((), ())), preferred_element_type=f32)
        lines = jnp.dot(placed.astype(bf16), yb_ref[...], preferred_element_type=f32)
        for part in range(2):
            a_ref[part] = lines[:, part * grid : (part + 1) * grid]

        for first in range(0, rows, 2):
            both = range(first, first + 2)
            high, low = [], []
            for plane in both:
                lines = jnp.concatenate([a_ref[part, pl.ds(plane, box, stride=rows), :] for part in range(2)], 0)
                high.append(lines.astype(bf16))
                low.append((lines - high[-1].astype(f32)).astype(bf16))
            high, low = jnp.concatenate(high, 1), jnp.concatenate(low, 1)
            field = jnp.dot(xb_ref[...], jnp.concatenate([high, high, low], 0), preferred_element_type=f32)
            weight = jnp.concatenate([pot_ref[plane] for plane in both], 1)
            field = (field * jnp.concatenate([weight, weight], 0)).astype(bf16)
            back = jnp.dot(xf_ref[...], field, preferred_element_type=f32)
            back = back[:pair] + back[pair:]
            for index, plane in enumerate(both):
                mine = back[:, index * grid : (index + 1) * grid]
                for part in range(2):
                    b_ref[part, pl.ds(plane, box, stride=rows), :] = mine[part * box : (part + 1) * box]

        lines = jnp.concatenate([b_ref[0], b_ref[1]], 1)
        high = lines.astype(bf16)
        low = (lines - high.astype(f32)).astype(bf16)
        boxed = jnp.dot(high, yf_ref[...], preferred_element_type=f32)
        boxed = boxed[:, :pair_pad] + boxed[:, pair_pad:]
        boxed = boxed + jnp.dot(low, yf_ref[:, :pair_pad], preferred_element_type=f32)
        boxed = boxed.astype(bf16)
        for part in range(2):
            for g in range(groups):
                where = part * sticks + g * local
                found = jnp.dot(boxed, hot_ref[0:pair_pad, where : where + local], preferred_element_type=f32)
                x_here = jnp.broadcast_to(x_rel[g : g + 1], (rows, local))
                total = jnp.zeros((rows, local), f32)
                for x in range(box):
                    total = total + jnp.where(x_here == float(x), found[x * rows : (x + 1) * rows], 0.0)
                out_ref[g, part * rows : (part + 1) * rows, :] = total.astype(bf16)

    return pl.pallas_call(
        kernel,
        out_shape=jax.ShapeDtypeStruct((groups, 2 * rows, local), bf16),
        in_specs=[vmem()] * 6,
        out_specs=vmem(),
        scratch_shapes=[
            pltpu.VMEM((box * rows, 2 * sticks), bf16),
            pltpu.VMEM((2 * pair_pad, 2 * sticks), bf16),
            pltpu.VMEM((2, box * rows, grid), f32),
            pltpu.VMEM((2, box * rows, grid), f32),
        ],
        name="apply_planes",
    )(received, potential, *[jnp.asarray(t) for t in (y_back, x_back, x_forward, y_forward)])


def image_sticks(sizes, columns, vector, positions):
    depth, local, grid = sizes.depth, sizes.sticks_local, sizes.grid
    height = 2 * depth

    def kernel(table_ref, columns_ref, vector_ref, position_ref, image_ref, rounded_ref, sums_ref):
        product = jnp.dot(table_ref[...], columns_ref[...], preferred_element_type=f32)
        applied = product[:height] + (product[height : 2 * height] + product[2 * height :])
        vector = vector_ref[...]
        x_freq = signed_freq(position_ref[...] // grid, grid)
        y_freq = signed_freq(position_ref[...] % grid, grid)
        row = lax.broadcasted_iota(jnp.int32, (height, local), 0)
        z_freq = jnp.where(row < depth, row, row - depth) - depth // 2
        kinetic = kinetic_unit * (z_freq * z_freq + (x_freq * x_freq + y_freq * y_freq)).astype(f32)
        image = kinetic * vector + applied
        image_ref[...] = image
        rounded_ref[0:height, :] = vector.astype(bf16)
        rounded_ref[height:, :] = image.astype(bf16)
        sums_ref[0:1, :] = jnp.sum(vector * image, axis=0, keepdims=True)
        sums_ref[1:2, :] = jnp.sum(vector * vector, axis=0, keepdims=True)

    return pl.pallas_call(
        kernel,
        out_shape=(
            jax.ShapeDtypeStruct((height, local), f32),
            jax.ShapeDtypeStruct((2 * height, local), bf16),
            jax.ShapeDtypeStruct((2, local), f32),
        ),
        in_specs=[vmem()] * 4,
        out_specs=(vmem(),) * 3,
        name="image_sticks",
    )(jnp.asarray(z_forward_table(sizes)), columns, vector, positions[None, :])


def shards(psi_res, correction, local_potential, stick_xy):
    groups = lax.axis_size("pw")
    planes, grid_size = local_potential.shape[:2]
    band_count, _, stick_depth, sticks_local = correction.shape
    res_count = psi_res.shape[0]
    sizes = Sizes(groups, planes, grid_size, stick_depth, sticks_local)
    length = stick_depth * sticks_local
    potential = jnp.pad(local_potential, ((0, sizes.rows - planes), (0, 0), (0, 0)))

    images, rounded, sums = [], [], []
    for band in range(band_count):
        vector = correction[band].reshape(2 * stick_depth, sticks_local)
        moving = spread_sticks(sizes, vector, stick_xy)
        moving = lax.all_to_all(moving, "pw", split_axis=0, concat_axis=0, tiled=True)
        picked = apply_planes(sizes, moving, potential)
        picked = lax.all_to_all(picked, "pw", split_axis=0, concat_axis=0, tiled=True)
        picked = picked.reshape(2 * sizes.rows * groups, sticks_local)
        one_image, one_rounded, one_sums = image_sticks(sizes, picked, vector, stick_xy)
        images.append(one_image)
        rounded.append(one_rounded)
        sums.append(one_sums)
    image = jnp.stack(images, 0).reshape(correction.shape)
    rounded = jnp.stack(rounded, 0)

    rows = lax.all_gather(rounded, "band", axis=0, tiled=True)
    row_count = rows.shape[0]
    rows = rows.reshape(row_count, 2, 2, length)
    straight = jnp.transpose(rows, (1, 0, 2, 3))
    turned = jnp.stack([straight[:, :, 1], -straight[:, :, 0]], 2)
    joined = jnp.stack([straight, turned], 1).reshape(4 * row_count, 2 * length)
    product = lax.dot_general(
        joined, psi_res.reshape(res_count, 2 * length), (((1,), (1,)), ((), ())), preferred_element_type=f32
    )
    flat = product.reshape(-1)
    tail = jnp.concatenate(sums, 0).reshape(-1)
    total_length = flat.shape[0] + tail.shape[0]
    padded = round_up(total_length, 8 * lanes)
    flat = jnp.concatenate([flat, tail, jnp.zeros((padded - total_length,), f32)]).reshape(-1, lanes)
    copies = jnp.broadcast_to(flat[None], (groups,) + flat.shape)
    copies = lax.all_to_all(copies, "pw", split_axis=0, concat_axis=0, tiled=True)
    total = jnp.sum(copies, axis=0).reshape(-1)
    product = total[: product.size].reshape(2, 2, row_count, res_count)
    product = jnp.transpose(product, (0, 1, 3, 2))
    tail = total[product.size : total_length].reshape(band_count, 2, sticks_local)
    tail = jnp.sum(tail, axis=2)
    rayleigh = tail[:, 0] / tail[:, 1]
    residual = image - rayleigh[:, None, None, None] * correction
    return (residual, product[1], product[0])


def solution(mesh):
    return jax.shard_map(
        shards,
        mesh=mesh,
        in_specs=(
            P("band", None, None, "pw"),
            P("band", None, None, "pw"),
            P("pw", None, None),
            P("pw"),
        ),
        out_specs=(P("band", None, None, "pw"), P(None, "band", None), P(None, "band", None)),
        check_vma=False,
    )
```

```python
import math

import jax
import jax.numpy as jnp
import numpy as np
from jax import lax
from jax.experimental import pallas as pl
from jax.experimental.pallas import tpu as pltpu
from jax.sharding import PartitionSpec as P

kinetic_unit = 0.002
highest = lax.Precision.HIGHEST
lanes = 128
f32 = jnp.float32
bf16 = jnp.bfloat16


def round_up(count, step):
    return -(-count // step) * step


def signed_freq(index, grid_size):
    return jnp.where(index < grid_size // 2, index, index - grid_size)


def phases(out_index, in_index, direction, grid_size):
    angles = (out_index[:, None] * in_index[None, :]) % grid_size * (2.0 * math.pi / grid_size)
    cosine, sine = np.cos(angles), direction * np.sin(angles)
    return np.stack([np.stack([cosine, -sine], 1), np.stack([sine, cosine], 1)], 0)


def split(table, count):
    pieces = []
    rest = np.asarray(table, np.float64)
    for _ in range(count):
        piece = rest.astype(jnp.bfloat16)
        pieces.append(piece)
        rest = rest - piece.astype(np.float64)
    return pieces


class Sizes:
    def __init__(self, groups, planes, grid_size, stick_depth, sticks_local):
        self.groups, self.planes = groups, planes
        self.grid, self.depth, self.sticks_local = grid_size, stick_depth, sticks_local
        self.rows = round_up(planes, 16)
        self.sticks = groups * sticks_local
        self.box = round_up(2 * math.ceil(math.sqrt(self.sticks / math.pi)) + 2, 8)
        self.line = round_up(self.box, 64)
        self.low_count = max(1, 256 // self.line)
        self.high_count = self.box // self.low_count


def z_rows(sizes):
    group = np.repeat(np.arange(sizes.groups), sizes.rows)
    plane = np.tile(np.arange(sizes.rows), sizes.groups)
    return group * sizes.planes + plane, plane < sizes.planes


def z_back_table(sizes):
    z_freq = np.arange(sizes.depth) - sizes.depth // 2
    z_index, real = z_rows(sizes)
    table = phases(z_index, z_freq, 1, sizes.grid) * real[None, :, None, None]
    table = table.reshape(2, sizes.groups, sizes.rows, 2 * sizes.depth)
    high, low = split(table.transpose(1, 0, 2, 3).reshape(-1, 2 * sizes.depth), 2)
    return np.concatenate([high, low, high], 1)


def z_forward_table(sizes):
    z_freq = np.arange(sizes.depth) - sizes.depth // 2
    z_index, real = z_rows(sizes)
    table = phases(z_freq, z_index, -1, sizes.grid) * real / float(sizes.grid**3)
    table = table.reshape(2 * sizes.depth, 2, sizes.groups, sizes.rows)
    table = table.transpose(0, 2, 1, 3).reshape(2 * sizes.depth, -1)
    return np.concatenate(split(table, 3), 0)


def plane_tables(sizes):
    grid = np.arange(sizes.grid)
    y_freq = np.arange(sizes.line) - sizes.box // 2
    order = np.arange(sizes.box).reshape(sizes.high_count, sizes.low_count).T.reshape(-1)
    x_freq = order - sizes.box // 2
    inside = np.arange(sizes.line) < sizes.box
    y_back = phases(grid, y_freq, 1, sizes.grid) * inside
    y_back = y_back.reshape(2 * sizes.grid, -1).T
    y_forward = phases(y_freq, grid, -1, sizes.grid) * inside[None, :, None, None]
    y_forward = y_forward.reshape(-1, 2 * sizes.grid).T
    x_back = phases(grid, x_freq, 1, sizes.grid).reshape(2 * sizes.grid, -1)
    x_forward = phases(x_freq, grid, -1, sizes.grid).reshape(-1, 2 * sizes.grid)
    y_back = np.concatenate(split(y_back, 2), 0)
    x_high, x_low = split(x_back, 2)
    x_back = np.concatenate([x_high, x_low, x_high], 1)
    x_forward = np.concatenate(split(x_forward, 2), 0)
    y_forward = np.concatenate(split(y_forward, 2), 1)
    return y_back, x_back, x_forward, y_forward


def call_on_chip(kernel, name, operands, shapes, scratch=()):
    spec = pl.BlockSpec(memory_space=pltpu.VMEM)
    return pl.pallas_call(
        kernel,
        out_shape=tuple(pltpu.VMEM(shape, dtype) for shape, dtype in shapes),
        in_specs=[spec] * len(operands),
        out_specs=(spec,) * len(shapes),
        scratch_shapes=list(scratch),
        name=name,
    )(*[pltpu.with_memory_space_constraint(operand, pltpu.VMEM) for operand in operands])


def spread_sticks(sizes, vector, positions):
    block = 2 * sizes.rows

    def kernel(table_ref, vector_ref, position_ref, out_ref):
        vector = vector_ref[...]
        high = vector.astype(bf16)
        low = (vector - high.astype(f32)).astype(bf16)
        stacked = jnp.concatenate([high, high, low], 0)
        columns = jnp.dot(table_ref[...], stacked, preferred_element_type=f32)
        x_pos = (position_ref[...] // sizes.grid).astype(f32)
        y_pos = (position_ref[...] % sizes.grid).astype(f32)
        row = lax.broadcasted_iota(jnp.int32, (16, sizes.sticks_local), 0)
        tail = jnp.where(row == 0, x_pos, jnp.where(row == 1, y_pos, 0.0)).astype(bf16)
        for group in range(sizes.groups):
            out_ref[group, 0:block, :] = columns[group * block : (group + 1) * block].astype(bf16)
            out_ref[group, block:, :] = tail

    return call_on_chip(
        kernel,
        "spread_sticks",
        (jnp.asarray(z_back_table(sizes)), vector, positions[None, :]),
        (((sizes.groups, block + 16, sizes.sticks_local), bf16),),
    )[0]


def turn(position, size):
    angle = (position - 0.5 * size) * (2.0 * math.pi / size)
    square = angle * angle
    cosine = jnp.zeros_like(angle)
    sine = jnp.zeros_like(angle)
    for order in range(7, -1, -1):
        sign = (-1.0) ** order
        cosine = cosine * square + sign / math.factorial(2 * order)
        sine = sine * square + sign / math.factorial(2 * order + 1)
    return -cosine, -sine * angle


def anchor_of(position, grid_size):
    spot = lax.broadcasted_iota(jnp.int32, (1, grid_size), 1).astype(f32)

    def total(values):
        return jnp.sum(jnp.sum(values, axis=0, keepdims=True), axis=1, keepdims=True)

    cosine, sine = turn(position, grid_size)
    spot_cosine, spot_sine = turn(spot, grid_size)
    score = total(cosine) * spot_cosine + total(sine) * spot_sine
    best = jnp.max(score, axis=1, keepdims=True)
    return jnp.min(jnp.where(score >= best, spot, float(grid_size)), axis=1, keepdims=True)


def cross(first, second, line):
    if line % lanes == 0:
        count = first.shape[1] // line
        return [
            jnp.concatenate([side[:, i * line : (i + 1) * line] for side in (first, second)], 1) for i in range(count)
        ]
    low = lax.broadcasted_iota(jnp.int32, (first.shape[0], lanes), 1) < line
    results = []
    for start in range(0, first.shape[1], lanes):
        one, two = first[:, start : start + lanes], second[:, start : start + lanes]
        results.append(jnp.where(low, one, pltpu.roll(two, line, 1)))
        results.append(jnp.where(low, pltpu.roll(one, line, 1), two))
    return results


def apply_planes(sizes, received, potential):
    grid, box, line, rows = sizes.grid, sizes.box, sizes.line, sizes.rows
    groups, local, sticks = sizes.groups, sizes.sticks_local, sizes.sticks
    low_count, high_count = sizes.low_count, sizes.high_count
    columns = low_count * line
    half = high_count * rows

    def kernel(in_ref, pot_ref, yb_ref, xb_ref, xf_ref, yf_ref, out_ref, left_ref, hot_ref, a_ref, b_ref):
        def relative(row):
            position = jnp.concatenate([in_ref[g, 2 * rows : 2 * rows + 16, :].astype(f32)[row : row + 1] for g in range(groups)], 0)
            moved = position - anchor_of(position, grid) + float(box // 2)
            moved = jnp.where(moved < 0, moved + float(grid), moved)
            return jnp.where(moved >= float(grid), moved - float(grid), moved)

        x_rel, y_rel = relative(0), relative(1)
        x_high = jnp.floor(x_rel * (1.0 / low_count))
        column = (x_rel - x_high * low_count) * float(line) + y_rel
        step = lax.broadcasted_iota(jnp.int32, (16, local), 0).astype(f32).astype(bf16)
        highs = []
        for g in range(groups):
            where = slice(g * local, (g + 1) * local)
            column_here = jnp.broadcast_to(column[g : g + 1], (16, local)).astype(bf16)
            for start in range(0, columns, 16):
                hot_ref[start : start + 16, where] = jnp.where(
                    column_here == step + jnp.asarray(start, bf16), jnp.asarray(1, bf16), jnp.asarray(0, bf16)
                )
            highs.append(jnp.broadcast_to(x_high[g : g + 1], (rows, local)))
            high_here = highs[g].astype(bf16)
            for part in range(2):
                values = in_ref[g, part * rows : (part + 1) * rows, :]
                for high in range(high_count):
                    start = (part * high_count + high) * rows
                    left_ref[start : start + rows, where] = jnp.where(
                        high_here == jnp.asarray(high, bf16), values, jnp.asarray(0, bf16)
                    )

        placed = lax.dot_general(left_ref[...], hot_ref[...], (((1,), (1,)), ((), ())), preferred_element_type=f32)
        placed = jnp.concatenate(cross(placed[:half], placed[half:], line), 0).astype(bf16)
        lines = jnp.dot(jnp.concatenate([placed, placed], 1), yb_ref[...], preferred_element_type=f32)
        for part in range(2):
            a_ref[part] = lines[:, part * grid : (part + 1) * grid]

        def to_field(first):
            high, low = [], []
            for plane in (first, first + 1):
                lines = jnp.concatenate([a_ref[part, pl.ds(plane, box, stride=rows), :] for part in range(2)], 0)
                high.append(lines.astype(bf16))
                low.append((lines - high[-1].astype(f32)).astype(bf16))
            high, low = jnp.concatenate(high, 1), jnp.concatenate(low, 1)
            field = jnp.dot(xb_ref[...], jnp.concatenate([high, high, low], 0), preferred_element_type=f32)
            weight = jnp.concatenate([pot_ref[first], pot_ref[first + 1]], 1)
            return (field * jnp.concatenate([weight, weight], 0)).astype(bf16)

        def from_field(first, field):
            back = jnp.dot(xf_ref[...], field, preferred_element_type=f32)
            back = back[: 2 * box] + back[2 * box :]
            for index in range(2):
                for part in range(2):
                    b_ref[part, pl.ds(first + index, box, stride=rows), :] = back[
                        part * box : (part + 1) * box, index * grid : (index + 1) * grid
                    ]

        fields = [to_field(0)]
        for first in range(0, rows, 2):
            if first + 2 < rows:
                fields.append(to_field(first + 2))
            from_field(first, fields[first // 2])

        lines = jnp.concatenate([b_ref[0], b_ref[1]], 1).astype(bf16)
        boxed = jnp.dot(lines, yf_ref[...], preferred_element_type=f32)
        boxed = boxed[:, : 2 * line] + boxed[:, 2 * line :]
        if line % lanes == 0:
            parts = [
                jnp.concatenate([boxed[low * half : (low + 1) * half, part * line : (part + 1) * line] for low in range(low_count)], 1)
                for part in range(2)
            ]
        else:
            pairs = [
                cross(boxed[low * half : (low + 1) * half], boxed[(low + 1) * half : (low + 2) * half], line)
                for low in range(0, low_count, 2)
            ]
            parts = [jnp.concatenate([pair[part] for pair in pairs], 1) for part in range(2)]
        boxed = jnp.concatenate(parts, 0).astype(bf16)
        for first in range(0, groups, 2):
            found = jnp.dot(boxed, hot_ref[:, first * local : (first + 2) * local], preferred_element_type=f32)
            for g in (first, first + 1):
                for part in range(2):
                    total = jnp.zeros((rows, local), f32)
                    for high in range(high_count):
                        start = (part * high_count + high) * rows
                        piece = found[start : start + rows, (g - first) * local : (g - first + 1) * local]
                        total = total + jnp.where(highs[g] == float(high), piece, 0.0)
                    out_ref[g, part * rows : (part + 1) * rows, :] = total.astype(bf16)

    return call_on_chip(
        kernel,
        "apply_planes",
        (received, potential, *[jnp.asarray(t) for t in plane_tables(sizes)]),
        (((groups, 2 * rows, local), bf16),),
        (
            pltpu.VMEM((2 * half, sticks), bf16),
            pltpu.VMEM((columns, sticks), bf16),
            pltpu.VMEM((2, box * rows, grid), f32),
            pltpu.VMEM((2, box * rows, grid), f32),
        ),
    )[0]


def image_sticks(sizes, columns, vector, positions):
    depth, local, grid = sizes.depth, sizes.sticks_local, sizes.grid
    height = 2 * depth

    def kernel(table_ref, columns_ref, vector_ref, position_ref, image_ref, rounded_ref, sums_ref):
        product = jnp.dot(table_ref[...], columns_ref[...], preferred_element_type=f32)
        applied = product[:height] + (product[height : 2 * height] + product[2 * height :])
        vector = vector_ref[...]
        x_freq = signed_freq(position_ref[...] // grid, grid)
        y_freq = signed_freq(position_ref[...] % grid, grid)
        row = lax.broadcasted_iota(jnp.int32, (height, local), 0)
        z_freq = jnp.where(row < depth, row, row - depth) - depth // 2
        kinetic = kinetic_unit * (z_freq * z_freq + (x_freq * x_freq + y_freq * y_freq)).astype(f32)
        image = kinetic * vector + applied
        image_ref[...] = image
        rounded_ref[0:height, :] = vector.astype(bf16)
        rounded_ref[height:, :] = image.astype(bf16)
        sums_ref[0:1, :] = jnp.sum(vector * image, axis=0, keepdims=True)
        sums_ref[1:2, :] = jnp.sum(vector * vector, axis=0, keepdims=True)

    return call_on_chip(
        kernel,
        "image_sticks",
        (jnp.asarray(z_forward_table(sizes)), columns, vector, positions[None, :]),
        (((height, local), f32), ((2 * height, local), bf16), ((2, local), f32)),
    )


def finish(copies, image, vector, band, band_total, res_count):
    count = copies.shape[0]
    width = 2 * res_count
    table = np.zeros((width, width), np.float32)
    lane = np.arange(width)
    table[lane, lane % 2 * res_count + lane // 2] = 1.0

    def kernel(band_ref, table_ref, copies_ref, image_ref, vector_ref, residual_ref, ham_ref, inter_ref, total_ref):
        total = copies_ref[0]
        for index in range(1, count):
            total = total + copies_ref[index]
        tail = jnp.sum(total[4 * band_total : 4 * band_total + 2], axis=1, keepdims=True)
        residual_ref[...] = image_ref[...] - (tail[0:1] / tail[1:2]) * vector_ref[...]
        total_ref[...] = jnp.dot(total[: 4 * band_total], table_ref[...], precision=highest, preferred_element_type=f32)
        for column in range(band_total):
            source = column ^ band_ref[0]
            for index, out_ref in enumerate((inter_ref, ham_ref)):
                real = total_ref[pl.ds(source * 4 + index * 2, 1), :]
                imag = total_ref[pl.ds(source * 4 + index * 2 + 1, 1), :]
                out_ref[0, column : column + 1, :] = real[:, :res_count] + imag[:, res_count:]
                out_ref[1, column : column + 1, :] = imag[:, :res_count] - real[:, res_count:]

    spec = pl.BlockSpec(memory_space=pltpu.VMEM)
    operands = (jnp.asarray(table), copies, image, vector)
    projection = jax.ShapeDtypeStruct((2, band_total, res_count), f32)
    return pl.pallas_call(
        kernel,
        out_shape=(jax.ShapeDtypeStruct(image.shape, f32), projection, projection),
        in_specs=[pl.BlockSpec(memory_space=pltpu.SMEM)] + [spec] * 4,
        out_specs=(spec,) * 3,
        scratch_shapes=[pltpu.VMEM((4 * band_total, width), f32)],
        name="finish",
    )(band, *[pltpu.with_memory_space_constraint(operand, pltpu.VMEM) for operand in operands])


def shards(psi_res, correction, local_potential, stick_xy):
    groups, band_total = lax.axis_size("pw"), lax.axis_size("band")
    planes, grid_size = local_potential.shape[:2]
    _, _, stick_depth, sticks_local = correction.shape
    res_count = psi_res.shape[0]
    sizes = Sizes(groups, planes, grid_size, stick_depth, sticks_local)
    potential = jnp.pad(local_potential, ((0, sizes.rows - planes), (0, 0), (0, 0)))
    vector = correction.reshape(2 * stick_depth, sticks_local)

    moving = spread_sticks(sizes, vector, stick_xy)
    moving = lax.all_to_all(moving, "pw", split_axis=0, concat_axis=0, tiled=True)
    picked = apply_planes(sizes, moving, potential)
    picked = lax.all_to_all(picked, "pw", split_axis=0, concat_axis=0, tiled=True)
    picked = picked.reshape(2 * sizes.rows * groups, sticks_local)
    image, rounded, sums = image_sticks(sizes, picked, vector, stick_xy)

    blocks = [rounded] + [
        lax.ppermute(rounded, "band", [(i, i ^ step) for i in range(band_total)]) for step in range(1, band_total)
    ]
    joined = jnp.concatenate(blocks, 0).reshape(4 * band_total, stick_depth, sticks_local)
    product = lax.dot_general(
        joined,
        psi_res.reshape(2 * res_count, stick_depth, sticks_local),
        (((1, 2), (1, 2)), ((), ())),
        preferred_element_type=f32,
    )
    height = round_up(4 * band_total + 2, 8)
    fill = jnp.zeros((height - 4 * band_total - 2, sticks_local), f32)
    partial = jnp.concatenate([product, sums, fill], 0)
    copies = jnp.broadcast_to(partial[None], (groups,) + partial.shape)
    copies = lax.all_to_all(copies, "pw", split_axis=0, concat_axis=0, tiled=True)
    band = lax.axis_index("band")[None]
    residual, hamiltonian, intersection = finish(copies, image, vector, band, band_total, res_count)
    return (
        residual.reshape(correction.shape),
        jnp.transpose(hamiltonian, (0, 2, 1)),
        jnp.transpose(intersection, (0, 2, 1)),
    )


def solution(mesh):
    return jax.shard_map(
        shards,
        mesh=mesh,
        in_specs=(
            P("band", None, None, "pw"),
            P("band", None, None, "pw"),
            P("pw", None, None),
            P("pw"),
        ),
        out_specs=(P("band", None, None, "pw"), P(None, "band", None), P(None, "band", None)),
        check_vma=False,
    )
```

```python
import math

import jax
import jax.numpy as jnp
import numpy as np
from jax import lax
from jax.experimental import pallas as pl
from jax.experimental.pallas import tpu as pltpu
from jax.sharding import PartitionSpec as P

kinetic_unit = 0.002
highest = lax.Precision.HIGHEST
lanes = 128
f32 = jnp.float32
bf16 = jnp.bfloat16


def round_up(count, step):
    return -(-count // step) * step


def signed_freq(index, grid_size):
    return jnp.where(index < grid_size // 2, index, index - grid_size)


def phases(out_index, in_index, direction, grid_size):
    angles = (out_index[:, None] * in_index[None, :]) % grid_size * (2.0 * math.pi / grid_size)
    cosine, sine = np.cos(angles), direction * np.sin(angles)
    return np.stack([np.stack([cosine, -sine], 1), np.stack([sine, cosine], 1)], 0)


def split(table, count):
    pieces = []
    rest = np.asarray(table, np.float64)
    for _ in range(count):
        piece = rest.astype(jnp.bfloat16)
        pieces.append(piece)
        rest = rest - piece.astype(np.float64)
    return pieces


class Sizes:
    def __init__(self, groups, planes, grid_size, stick_depth, sticks_local):
        self.groups, self.planes = groups, planes
        self.grid, self.depth, self.sticks_local = grid_size, stick_depth, sticks_local
        self.rows = round_up(planes, 16)
        self.sticks = groups * sticks_local
        self.box = round_up(2 * math.ceil(math.sqrt(self.sticks / math.pi)) + 2, 8)
        self.line = round_up(self.box, 64)
        self.low_count = max(1, 256 // self.line)
        self.high_count = self.box // self.low_count


def z_rows(sizes):
    group = np.repeat(np.arange(sizes.groups), sizes.rows)
    plane = np.tile(np.arange(sizes.rows), sizes.groups)
    return group * sizes.planes + plane, plane < sizes.planes


def z_back_table(sizes):
    z_freq = np.arange(sizes.depth) - sizes.depth // 2
    z_index, real = z_rows(sizes)
    table = phases(z_index, z_freq, 1, sizes.grid) * real[None, :, None, None]
    table = table.reshape(2, sizes.groups, sizes.rows, 2 * sizes.depth)
    high, low = split(table.transpose(1, 0, 2, 3).reshape(-1, 2 * sizes.depth), 2)
    return np.concatenate([high, low, high], 1)


def z_forward_table(sizes):
    z_freq = np.arange(sizes.depth) - sizes.depth // 2
    z_index, real = z_rows(sizes)
    table = phases(z_freq, z_index, -1, sizes.grid) * real / float(sizes.grid**3)
    table = table.reshape(2 * sizes.depth, 2, sizes.groups, sizes.rows)
    table = table.transpose(0, 2, 1, 3).reshape(2 * sizes.depth, -1)
    return np.concatenate(split(table, 3), 0)


def plane_tables(sizes):
    grid = np.arange(sizes.grid)
    y_freq = np.arange(sizes.line) - sizes.box // 2
    order = np.arange(sizes.box).reshape(sizes.high_count, sizes.low_count).T.reshape(-1)
    x_freq = order - sizes.box // 2
    inside = np.arange(sizes.line) < sizes.box
    y_back = phases(grid, y_freq, 1, sizes.grid) * inside
    y_back = y_back.reshape(2 * sizes.grid, -1).T
    y_forward = phases(y_freq, grid, -1, sizes.grid) * inside[None, :, None, None]
    y_forward = y_forward.reshape(-1, 2 * sizes.grid).T
    x_back = phases(grid, x_freq, 1, sizes.grid).reshape(2 * sizes.grid, -1)
    x_forward = phases(x_freq, grid, -1, sizes.grid).reshape(-1, 2 * sizes.grid)
    y_back = np.concatenate(split(y_back, 2), 0)
    x_high, x_low = split(x_back, 2)
    x_back = np.concatenate([x_high, x_low, x_high], 1)
    x_forward = np.concatenate(split(x_forward, 2), 0)
    y_forward = np.concatenate(split(y_forward, 2), 1)
    return y_back, x_back, x_forward, y_forward


def call_on_chip(kernel, name, operands, shapes, far=(), scratch=()):
    spec = pl.BlockSpec(memory_space=pltpu.VMEM)
    return pl.pallas_call(
        kernel,
        out_shape=tuple(pltpu.VMEM(shape, dtype) for shape, dtype in shapes),
        in_specs=[spec] * len(operands) + [pl.BlockSpec(memory_space=pl.ANY)] * len(far),
        out_specs=(spec,) * len(shapes),
        scratch_shapes=list(scratch),
        name=name,
    )(*[pltpu.with_memory_space_constraint(operand, pltpu.VMEM) for operand in operands], *far)


def spread_sticks(sizes, vector, positions):
    block = 2 * sizes.rows
    far = (jnp.asarray(z_back_table(sizes)), vector, positions[None, :])

    def kernel(table_far, vector_far, position_far, out_ref, table_ref, vector_ref, position_ref, sems):
        pairs = ((vector_far, vector_ref), (table_far, table_ref), (position_far, position_ref))
        copies = [pltpu.make_async_copy(far, near, sems.at[index]) for index, (far, near) in enumerate(pairs)]
        for copy in copies:
            copy.start()
        for copy in copies:
            copy.wait()
        vector = vector_ref[...]
        high = vector.astype(bf16)
        low = (vector - high.astype(f32)).astype(bf16)
        stacked = jnp.concatenate([high, high, low], 0)
        columns = jnp.dot(table_ref[...], stacked, preferred_element_type=f32)
        x_pos = (position_ref[...] // sizes.grid).astype(f32)
        y_pos = (position_ref[...] % sizes.grid).astype(f32)
        row = lax.broadcasted_iota(jnp.int32, (16, sizes.sticks_local), 0)
        tail = jnp.where(row == 0, x_pos, jnp.where(row == 1, y_pos, 0.0)).astype(bf16)
        for group in range(sizes.groups):
            out_ref[group, 0:block, :] = columns[group * block : (group + 1) * block].astype(bf16)
            out_ref[group, block:, :] = tail

    return call_on_chip(
        kernel,
        "spread_sticks",
        (),
        (((sizes.groups, block + 16, sizes.sticks_local), bf16),),
        far,
        [pltpu.VMEM(operand.shape, operand.dtype) for operand in far] + [pltpu.SemaphoreType.DMA((3,))],
    )[0]


def turn(position, size):
    angle = (position - 0.5 * size) * (2.0 * math.pi / size)
    square = angle * angle
    cosine = jnp.zeros_like(angle)
    sine = jnp.zeros_like(angle)
    for order in range(7, -1, -1):
        sign = (-1.0) ** order
        cosine = cosine * square + sign / math.factorial(2 * order)
        sine = sine * square + sign / math.factorial(2 * order + 1)
    return -cosine, -sine * angle


def anchor_of(position, grid_size):
    spot = lax.broadcasted_iota(jnp.int32, (1, grid_size), 1).astype(f32)

    def total(values):
        return jnp.sum(jnp.sum(values, axis=0, keepdims=True), axis=1, keepdims=True)

    cosine, sine = turn(position, grid_size)
    spot_cosine, spot_sine = turn(spot, grid_size)
    score = total(cosine) * spot_cosine + total(sine) * spot_sine
    best = jnp.max(score, axis=1, keepdims=True)
    return jnp.min(jnp.where(score >= best, spot, float(grid_size)), axis=1, keepdims=True)


def cross(first, second, line):
    if line % lanes == 0:
        count = first.shape[1] // line
        return [
            jnp.concatenate([side[:, i * line : (i + 1) * line] for side in (first, second)], 1) for i in range(count)
        ]
    low = lax.broadcasted_iota(jnp.int32, (first.shape[0], lanes), 1) < line
    results = []
    for start in range(0, first.shape[1], lanes):
        one, two = first[:, start : start + lanes], second[:, start : start + lanes]
        results.append(jnp.where(low, one, pltpu.roll(two, line, 1)))
        results.append(jnp.where(low, pltpu.roll(one, line, 1), two))
    return results


def apply_planes(sizes, received, potential, psi_res):
    far = (*[jnp.asarray(t) for t in plane_tables(sizes)], potential, psi_res)
    grid, box, line, rows = sizes.grid, sizes.box, sizes.line, sizes.rows
    groups, local, sticks = sizes.groups, sizes.sticks_local, sizes.sticks
    low_count, high_count = sizes.low_count, sizes.high_count
    columns = low_count * line
    half = high_count * rows

    def kernel(in_ref, *refs):
        distant, (out_ref, psi_ref), near = refs[:6], refs[6:8], refs[8:13]
        left_ref, hot_ref, a_ref, b_ref, sems = refs[13:]
        yb_ref, xb_ref, xf_ref, yf_ref, pot_ref = near
        copies = [
            pltpu.make_async_copy(source, target, sems.at[index])
            for index, (source, target) in enumerate(zip(distant, (*near, psi_ref), strict=True))
        ]
        yb_copy, xb_copy, xf_copy, yf_copy, pot_copy, psi_copy = copies
        for copy in copies:
            copy.start()

        def relative(row):
            position = jnp.concatenate([in_ref[g, 2 * rows : 2 * rows + 16, :].astype(f32)[row : row + 1] for g in range(groups)], 0)
            moved = position - anchor_of(position, grid) + float(box // 2)
            moved = jnp.where(moved < 0, moved + float(grid), moved)
            return jnp.where(moved >= float(grid), moved - float(grid), moved)

        x_rel, y_rel = relative(0), relative(1)
        x_high = jnp.floor(x_rel * (1.0 / low_count))
        column = (x_rel - x_high * low_count) * float(line) + y_rel
        step = lax.broadcasted_iota(jnp.int32, (16, local), 0).astype(f32).astype(bf16)
        highs = []
        for g in range(groups):
            where = slice(g * local, (g + 1) * local)
            column_here = jnp.broadcast_to(column[g : g + 1], (16, local)).astype(bf16)
            for start in range(0, columns, 16):
                hot_ref[start : start + 16, where] = jnp.where(
                    column_here == step + jnp.asarray(start, bf16), jnp.asarray(1, bf16), jnp.asarray(0, bf16)
                )
            highs.append(jnp.broadcast_to(x_high[g : g + 1], (rows, local)))
            high_here = highs[g].astype(bf16)
            for part in range(2):
                values = in_ref[g, part * rows : (part + 1) * rows, :]
                for high in range(high_count):
                    start = (part * high_count + high) * rows
                    left_ref[start : start + rows, where] = jnp.where(
                        high_here == jnp.asarray(high, bf16), values, jnp.asarray(0, bf16)
                    )

        placed = lax.dot_general(left_ref[...], hot_ref[...], (((1,), (1,)), ((), ())), preferred_element_type=f32)
        yb_copy.wait()
        placed = jnp.concatenate(cross(placed[:half], placed[half:], line), 0).astype(bf16)
        lines = jnp.dot(jnp.concatenate([placed, placed], 1), yb_ref[...], preferred_element_type=f32)
        for part in range(2):
            a_ref[part] = lines[:, part * grid : (part + 1) * grid]

        def to_field(first):
            high, low = [], []
            for plane in (first, first + 1):
                lines = jnp.concatenate([a_ref[part, pl.ds(plane, box, stride=rows), :] for part in range(2)], 0)
                high.append(lines.astype(bf16))
                low.append((lines - high[-1].astype(f32)).astype(bf16))
            high, low = jnp.concatenate(high, 1), jnp.concatenate(low, 1)
            field = jnp.dot(xb_ref[...], jnp.concatenate([high, high, low], 0), preferred_element_type=f32)
            weight = jnp.concatenate([pot_ref[first], pot_ref[first + 1]], 1)
            return (field * jnp.concatenate([weight, weight], 0)).astype(bf16)

        def from_field(first, field):
            back = jnp.dot(xf_ref[...], field, preferred_element_type=f32)
            back = back[: 2 * box] + back[2 * box :]
            for index in range(2):
                for part in range(2):
                    b_ref[part, pl.ds(first + index, box, stride=rows), :] = back[
                        part * box : (part + 1) * box, index * grid : (index + 1) * grid
                    ]

        for copy in (xb_copy, pot_copy, xf_copy):
            copy.wait()
        fields = [to_field(0)]
        for first in range(0, rows, 2):
            if first + 2 < rows:
                fields.append(to_field(first + 2))
            from_field(first, fields[first // 2])

        yf_copy.wait()
        lines = jnp.concatenate([b_ref[0], b_ref[1]], 1).astype(bf16)
        boxed = jnp.dot(lines, yf_ref[...], preferred_element_type=f32)
        boxed = boxed[:, : 2 * line] + boxed[:, 2 * line :]
        if line % lanes == 0:
            parts = [
                jnp.concatenate([boxed[low * half : (low + 1) * half, part * line : (part + 1) * line] for low in range(low_count)], 1)
                for part in range(2)
            ]
        else:
            pairs = [
                cross(boxed[low * half : (low + 1) * half], boxed[(low + 1) * half : (low + 2) * half], line)
                for low in range(0, low_count, 2)
            ]
            parts = [jnp.concatenate([pair[part] for pair in pairs], 1) for part in range(2)]
        boxed = jnp.concatenate(parts, 0).astype(bf16)
        for first in range(0, groups, 2):
            found = jnp.dot(boxed, hot_ref[:, first * local : (first + 2) * local], preferred_element_type=f32)
            for g in (first, first + 1):
                for part in range(2):
                    total = jnp.zeros((rows, local), f32)
                    for high in range(high_count):
                        start = (part * high_count + high) * rows
                        piece = found[start : start + rows, (g - first) * local : (g - first + 1) * local]
                        total = total + jnp.where(highs[g] == float(high), piece, 0.0)
                    out_ref[g, part * rows : (part + 1) * rows, :] = total.astype(bf16)
        psi_copy.wait()

    return call_on_chip(
        kernel,
        "apply_planes",
        (received,),
        (((groups, 2 * rows, local), bf16), (psi_res.shape, psi_res.dtype)),
        far,
        (
            *[pltpu.VMEM(operand.shape, operand.dtype) for operand in far[:5]],
            pltpu.VMEM((2 * half, sticks), bf16),
            pltpu.VMEM((columns, sticks), bf16),
            pltpu.VMEM((2, box * rows, grid), f32),
            pltpu.VMEM((2, box * rows, grid), f32),
            pltpu.SemaphoreType.DMA((6,)),
        ),
    )


def image_sticks(sizes, columns, vector, positions):
    depth, local, grid = sizes.depth, sizes.sticks_local, sizes.grid
    height = 2 * depth

    def kernel(table_ref, columns_ref, vector_ref, position_ref, image_ref, rounded_ref, sums_ref):
        product = jnp.dot(table_ref[...], columns_ref[...], preferred_element_type=f32)
        applied = product[:height] + (product[height : 2 * height] + product[2 * height :])
        vector = vector_ref[...]
        x_freq = signed_freq(position_ref[...] // grid, grid)
        y_freq = signed_freq(position_ref[...] % grid, grid)
        row = lax.broadcasted_iota(jnp.int32, (height, local), 0)
        z_freq = jnp.where(row < depth, row, row - depth) - depth // 2
        kinetic = kinetic_unit * (z_freq * z_freq + (x_freq * x_freq + y_freq * y_freq)).astype(f32)
        image = kinetic * vector + applied
        image_ref[...] = image
        rounded_ref[0:height, :] = vector.astype(bf16)
        rounded_ref[height:, :] = image.astype(bf16)
        sums_ref[0:1, :] = jnp.sum(vector * image, axis=0, keepdims=True)
        sums_ref[1:2, :] = jnp.sum(vector * vector, axis=0, keepdims=True)

    return call_on_chip(
        kernel,
        "image_sticks",
        (jnp.asarray(z_forward_table(sizes)), columns, vector, positions[None, :]),
        (((height, local), f32), ((2 * height, local), bf16), ((2, local), f32)),
    )


def share(product, sums, groups):
    count, width = product.shape
    height = round_up(count + 2, 8)

    def kernel(product_ref, sums_ref, out_ref):
        fill = jnp.zeros((height - count - 2, width), f32)
        partial = jnp.concatenate([product_ref[...], sums_ref[...], fill], 0)
        for group in range(groups):
            out_ref[group] = partial

    return call_on_chip(kernel, "share", (product, sums), (((groups, height, width), f32),))[0]


def finish(copies, image, vector, band, band_total, res_count):
    count = copies.shape[0]
    width = 2 * res_count
    table = np.zeros((width, width), np.float32)
    lane = np.arange(width)
    table[lane, lane % 2 * res_count + lane // 2] = 1.0

    def kernel(band_ref, table_ref, copies_ref, image_ref, vector_ref, residual_ref, ham_ref, inter_ref, total_ref):
        total = copies_ref[0]
        for index in range(1, count):
            total = total + copies_ref[index]
        tail = jnp.sum(total[4 * band_total : 4 * band_total + 2], axis=1, keepdims=True)
        residual_ref[...] = image_ref[...] - (tail[0:1] / tail[1:2]) * vector_ref[...]
        total_ref[...] = jnp.dot(total[: 4 * band_total], table_ref[...], precision=highest, preferred_element_type=f32)
        for column in range(band_total):
            source = column ^ band_ref[0]
            for index, out_ref in enumerate((inter_ref, ham_ref)):
                real = total_ref[pl.ds(source * 4 + index * 2, 1), :]
                imag = total_ref[pl.ds(source * 4 + index * 2 + 1, 1), :]
                out_ref[0, column : column + 1, :] = real[:, :res_count] + imag[:, res_count:]
                out_ref[1, column : column + 1, :] = imag[:, :res_count] - real[:, res_count:]

    spec = pl.BlockSpec(memory_space=pltpu.VMEM)
    operands = (jnp.asarray(table), copies, image, vector)
    projection = jax.ShapeDtypeStruct((2, band_total, res_count), f32)
    return pl.pallas_call(
        kernel,
        out_shape=(jax.ShapeDtypeStruct(image.shape, f32), projection, projection),
        in_specs=[pl.BlockSpec(memory_space=pltpu.SMEM)] + [spec] * 4,
        out_specs=(spec,) * 3,
        scratch_shapes=[pltpu.VMEM((4 * band_total, width), f32)],
        name="finish",
    )(band, *[pltpu.with_memory_space_constraint(operand, pltpu.VMEM) for operand in operands])


def shards(psi_res, correction, local_potential, stick_xy):
    groups, band_total = lax.axis_size("pw"), lax.axis_size("band")
    planes, grid_size = local_potential.shape[:2]
    _, _, stick_depth, sticks_local = correction.shape
    res_count = psi_res.shape[0]
    sizes = Sizes(groups, planes, grid_size, stick_depth, sticks_local)
    potential = jnp.pad(local_potential, ((0, sizes.rows - planes), (0, 0), (0, 0)))
    vector = correction.reshape(2 * stick_depth, sticks_local)

    moving = spread_sticks(sizes, vector, stick_xy)
    moving = lax.all_to_all(moving, "pw", split_axis=0, concat_axis=0, tiled=True)
    picked, psi_near = apply_planes(sizes, moving, potential, psi_res.reshape(2 * res_count, stick_depth, sticks_local))
    picked = lax.all_to_all(picked, "pw", split_axis=0, concat_axis=0, tiled=True)
    picked = picked.reshape(2 * sizes.rows * groups, sticks_local)
    image, rounded, sums = image_sticks(sizes, picked, vector, stick_xy)

    blocks = [rounded] + [
        lax.ppermute(rounded, "band", [(i, i ^ step) for i in range(band_total)]) for step in range(1, band_total)
    ]
    joined = jnp.concatenate(blocks, 0).reshape(4 * band_total, stick_depth, sticks_local)
    product = lax.dot_general(
        joined,
        psi_near,
        (((1, 2), (1, 2)), ((), ())),
        preferred_element_type=f32,
    )
    copies = share(product, sums, groups)
    copies = lax.all_to_all(copies, "pw", split_axis=0, concat_axis=0, tiled=True)
    band = lax.axis_index("band")[None]
    residual, hamiltonian, intersection = finish(copies, image, vector, band, band_total, res_count)
    return (
        residual.reshape(correction.shape),
        jnp.transpose(hamiltonian, (0, 2, 1)),
        jnp.transpose(intersection, (0, 2, 1)),
    )


def solution(mesh):
    return jax.shard_map(
        shards,
        mesh=mesh,
        in_specs=(
            P("band", None, None, "pw"),
            P("band", None, None, "pw"),
            P("pw", None, None),
            P("pw"),
        ),
        out_specs=(P("band", None, None, "pw"), P(None, "band", None), P(None, "band", None)),
        check_vma=False,
    )
```

```python
import math

import jax
import jax.numpy as jnp
import numpy as np
from jax import lax
from jax.experimental import pallas as pl
from jax.experimental.pallas import tpu as pltpu
from jax.sharding import PartitionSpec as P

kinetic_unit = 0.002
highest = lax.Precision.HIGHEST
lanes = 128
f32 = jnp.float32
bf16 = jnp.bfloat16


def round_up(count, step):
    return -(-count // step) * step


def signed_freq(index, grid_size):
    return jnp.where(index < grid_size // 2, index, index - grid_size)


def phases(out_index, in_index, direction, grid_size):
    angles = (out_index[:, None] * in_index[None, :]) % grid_size * (2.0 * math.pi / grid_size)
    cosine, sine = np.cos(angles), direction * np.sin(angles)
    return np.stack([np.stack([cosine, -sine], 1), np.stack([sine, cosine], 1)], 0)


def split(table, count):
    pieces = []
    rest = np.asarray(table, np.float64)
    for _ in range(count):
        piece = rest.astype(jnp.bfloat16)
        pieces.append(piece)
        rest = rest - piece.astype(np.float64)
    return pieces


class Sizes:
    def __init__(self, groups, planes, grid_size, stick_depth, sticks_local):
        self.groups, self.planes = groups, planes
        self.grid, self.depth, self.sticks_local = grid_size, stick_depth, sticks_local
        self.rows = round_up(planes, 16)
        self.sticks = groups * sticks_local
        self.box = round_up(2 * math.ceil(math.sqrt(self.sticks / math.pi)) + 2, 8)
        self.line = round_up(self.box, 64)
        self.low_count = max(1, 256 // self.line)
        self.high_count = self.box // self.low_count


def z_rows(sizes):
    group = np.repeat(np.arange(sizes.groups), sizes.rows)
    plane = np.tile(np.arange(sizes.rows), sizes.groups)
    return group * sizes.planes + plane, plane < sizes.planes


def z_back_table(sizes):
    z_freq = np.arange(sizes.depth) - sizes.depth // 2
    z_index, real = z_rows(sizes)
    table = phases(z_index, z_freq, 1, sizes.grid) * real[None, :, None, None]
    table = table.reshape(2, sizes.groups, sizes.rows, 2 * sizes.depth)
    high, low = split(table.transpose(1, 0, 2, 3).reshape(-1, 2 * sizes.depth), 2)
    return np.concatenate([high, low, high], 1)


def z_forward_table(sizes):
    z_freq = np.arange(sizes.depth) - sizes.depth // 2
    z_index, real = z_rows(sizes)
    table = phases(z_freq, z_index, -1, sizes.grid) * real / float(sizes.grid**3)
    table = table.reshape(2 * sizes.depth, 2, sizes.groups, sizes.rows)
    table = table.transpose(0, 2, 1, 3).reshape(2 * sizes.depth, -1)
    return np.concatenate(split(table, 3), 0)


def plane_tables(sizes):
    grid = np.arange(sizes.grid)
    y_freq = np.arange(sizes.line) - sizes.box // 2
    order = np.arange(sizes.box).reshape(sizes.high_count, sizes.low_count).T.reshape(-1)
    x_freq = order - sizes.box // 2
    inside = np.arange(sizes.line) < sizes.box
    y_back = phases(grid, y_freq, 1, sizes.grid) * inside
    y_back = y_back.reshape(2 * sizes.grid, -1).T
    y_forward = phases(y_freq, grid, -1, sizes.grid) * inside[None, :, None, None]
    y_forward = y_forward.reshape(-1, 2 * sizes.grid).T
    x_back = phases(grid, x_freq, 1, sizes.grid).reshape(2 * sizes.grid, -1)
    x_forward = phases(x_freq, grid, -1, sizes.grid).reshape(-1, 2 * sizes.grid)
    y_back = np.concatenate(split(y_back, 2), 0)
    x_high, x_low = split(x_back, 2)
    x_back = np.concatenate([x_high, x_low, x_high], 1)
    x_forward = np.concatenate(split(x_forward, 2), 0)
    y_forward = np.concatenate(split(y_forward, 2), 1)
    return y_back, x_back, x_forward, y_forward


def call_on_chip(kernel, name, operands, shapes, far=(), scratch=()):
    spec = pl.BlockSpec(memory_space=pltpu.VMEM)
    return pl.pallas_call(
        kernel,
        out_shape=tuple(pltpu.VMEM(shape, dtype) for shape, dtype in shapes),
        in_specs=[spec] * len(operands) + [pl.BlockSpec(memory_space=pl.ANY)] * len(far),
        out_specs=(spec,) * len(shapes),
        scratch_shapes=list(scratch),
        name=name,
    )(*[pltpu.with_memory_space_constraint(operand, pltpu.VMEM) for operand in operands], *far)


def spread_sticks(sizes, vector, positions, y_back):
    block = 2 * sizes.rows
    z_table = jnp.asarray(z_back_table(sizes))
    kept = (vector, positions[None, :], y_back)
    far = (kept[0], z_table, *kept[1:])

    def kernel(*refs):
        distant, (out_ref, *near), (table_ref, sems) = refs[: len(far)], refs[len(far) : -2], refs[-2:]
        vector_ref, position_ref = near[:2]
        copies = [
            pltpu.make_async_copy(source, target, sems.at[index])
            for index, (source, target) in enumerate(zip(distant, (near[0], table_ref, *near[1:]), strict=True))
        ]
        for copy in copies:
            copy.start()
        for copy in copies[:3]:
            copy.wait()
        vector = vector_ref[...]
        high = vector.astype(bf16)
        low = (vector - high.astype(f32)).astype(bf16)
        stacked = jnp.concatenate([high, high, low], 0)
        columns = jnp.dot(table_ref[...], stacked, preferred_element_type=f32)
        x_pos = (position_ref[...] // sizes.grid).astype(f32)
        y_pos = (position_ref[...] % sizes.grid).astype(f32)
        row = lax.broadcasted_iota(jnp.int32, (16, sizes.sticks_local), 0)
        tail = jnp.where(row == 0, x_pos, jnp.where(row == 1, y_pos, 0.0)).astype(bf16)
        for group in range(sizes.groups):
            out_ref[group, 0:block, :] = columns[group * block : (group + 1) * block].astype(bf16)
            out_ref[group, block:, :] = tail
        for copy in copies[3:]:
            copy.wait()

    return call_on_chip(
        kernel,
        "spread_sticks",
        (),
        (((sizes.groups, block + 16, sizes.sticks_local), bf16), *[(array.shape, array.dtype) for array in kept]),
        far,
        [pltpu.VMEM(z_table.shape, z_table.dtype), pltpu.SemaphoreType.DMA((len(far),))],
    )


def turn(position, size):
    angle = (position - 0.5 * size) * (2.0 * math.pi / size)
    square = angle * angle
    cosine = jnp.zeros_like(angle)
    sine = jnp.zeros_like(angle)
    for order in range(7, -1, -1):
        sign = (-1.0) ** order
        cosine = cosine * square + sign / math.factorial(2 * order)
        sine = sine * square + sign / math.factorial(2 * order + 1)
    return -cosine, -sine * angle


def anchor_of(position, grid_size):
    spot = lax.broadcasted_iota(jnp.int32, (1, grid_size), 1).astype(f32)

    def total(values):
        return jnp.sum(jnp.sum(values, axis=0, keepdims=True), axis=1, keepdims=True)

    cosine, sine = turn(position, grid_size)
    spot_cosine, spot_sine = turn(spot, grid_size)
    score = total(cosine) * spot_cosine + total(sine) * spot_sine
    best = jnp.max(score, axis=1, keepdims=True)
    return jnp.min(jnp.where(score >= best, spot, float(grid_size)), axis=1, keepdims=True)


def cross(first, second, line):
    if line % lanes == 0:
        count = first.shape[1] // line
        return [
            jnp.concatenate([side[:, i * line : (i + 1) * line] for side in (first, second)], 1) for i in range(count)
        ]
    low = lax.broadcasted_iota(jnp.int32, (first.shape[0], lanes), 1) < line
    results = []
    for start in range(0, first.shape[1], lanes):
        one, two = first[:, start : start + lanes], second[:, start : start + lanes]
        results.append(jnp.where(low, one, pltpu.roll(two, line, 1)))
        results.append(jnp.where(low, pltpu.roll(one, line, 1), two))
    return results


def apply_planes(sizes, received, near, later, psi_res):
    grid, box, line, rows = sizes.grid, sizes.box, sizes.line, sizes.rows
    groups, local, sticks = sizes.groups, sizes.sticks_local, sizes.sticks
    low_count, high_count = sizes.low_count, sizes.high_count
    columns = low_count * line
    half = high_count * rows

    psi_bytes, other_bytes = (sum(array.nbytes for array in arrays) for arrays in ((psi_res,), (received, received, near)))
    bring = psi_bytes + other_bytes < 3200000

    def kernel(in_ref, yb_ref, *refs):
        *distant, out_ref = refs[:5]
        scratch = refs[5:]
        if bring:
            *distant, psi_far = refs[:5]
            out_ref, psi_ref, *scratch = refs[5:]
        *near_refs, left_ref, hot_ref, a_ref, b_ref, sems = scratch
        xb_ref, pot_ref, xf_ref, yf_ref = near_refs
        copies = [
            pltpu.make_async_copy(source, target, sems.at[index])
            for index, (source, target) in enumerate(zip(distant, near_refs, strict=True))
        ]
        if bring:
            copies.append(pltpu.make_async_copy(psi_far, psi_ref, sems.at[4]))
        for copy in copies:
            copy.start()

        def relative(row):
            position = jnp.concatenate([in_ref[g, 2 * rows : 2 * rows + 16, :].astype(f32)[row : row + 1] for g in range(groups)], 0)
            moved = position - anchor_of(position, grid) + float(box // 2)
            moved = jnp.where(moved < 0, moved + float(grid), moved)
            return jnp.where(moved >= float(grid), moved - float(grid), moved)

        x_rel, y_rel = relative(0), relative(1)
        x_high = jnp.floor(x_rel * (1.0 / low_count))
        column = (x_rel - x_high * low_count) * float(line) + y_rel
        step = lax.broadcasted_iota(jnp.int32, (16, local), 0).astype(f32).astype(bf16)
        highs = []
        for g in range(groups):
            where = slice(g * local, (g + 1) * local)
            column_here = jnp.broadcast_to(column[g : g + 1], (16, local)).astype(bf16)
            for start in range(0, columns, 16):
                hot_ref[start : start + 16, where] = jnp.where(
                    column_here == step + jnp.asarray(start, bf16), jnp.asarray(1, bf16), jnp.asarray(0, bf16)
                )
            highs.append(jnp.broadcast_to(x_high[g : g + 1], (rows, local)))
            high_here = highs[g].astype(bf16)
            for part in range(2):
                values = in_ref[g, part * rows : (part + 1) * rows, :]
                for high in range(high_count):
                    start = (part * high_count + high) * rows
                    left_ref[start : start + rows, where] = jnp.where(
                        high_here == jnp.asarray(high, bf16), values, jnp.asarray(0, bf16)
                    )

        placed = lax.dot_general(left_ref[...], hot_ref[...], (((1,), (1,)), ((), ())), preferred_element_type=f32)
        placed = jnp.concatenate(cross(placed[:half], placed[half:], line), 0).astype(bf16)
        lines = jnp.dot(jnp.concatenate([placed, placed], 1), yb_ref[...], preferred_element_type=f32)
        for part in range(2):
            a_ref[part] = lines[:, part * grid : (part + 1) * grid]

        def to_field(first):
            high, low = [], []
            for plane in (first, first + 1):
                lines = jnp.concatenate([a_ref[part, pl.ds(plane, box, stride=rows), :] for part in range(2)], 0)
                high.append(lines.astype(bf16))
                low.append((lines - high[-1].astype(f32)).astype(bf16))
            high, low = jnp.concatenate(high, 1), jnp.concatenate(low, 1)
            field = jnp.dot(xb_ref[...], jnp.concatenate([high, high, low], 0), preferred_element_type=f32)
            weight = jnp.concatenate([pot_ref[first], pot_ref[first + 1]], 1)
            return (field * jnp.concatenate([weight, weight], 0)).astype(bf16)

        def from_field(first, field):
            back = jnp.dot(xf_ref[...], field, preferred_element_type=f32)
            back = back[: 2 * box] + back[2 * box :]
            for index in range(2):
                for part in range(2):
                    b_ref[part, pl.ds(first + index, box, stride=rows), :] = back[
                        part * box : (part + 1) * box, index * grid : (index + 1) * grid
                    ]

        for copy in copies[:3]:
            copy.wait()
        fields = [to_field(0)]
        for first in range(0, rows, 2):
            if first + 2 < rows:
                fields.append(to_field(first + 2))
            from_field(first, fields[first // 2])

        copies[3].wait()
        lines = jnp.concatenate([b_ref[0], b_ref[1]], 1).astype(bf16)
        boxed = jnp.dot(lines, yf_ref[...], preferred_element_type=f32)
        boxed = boxed[:, : 2 * line] + boxed[:, 2 * line :]
        if line % lanes == 0:
            parts = [
                jnp.concatenate([boxed[low * half : (low + 1) * half, part * line : (part + 1) * line] for low in range(low_count)], 1)
                for part in range(2)
            ]
        else:
            pairs = [
                cross(boxed[low * half : (low + 1) * half], boxed[(low + 1) * half : (low + 2) * half], line)
                for low in range(0, low_count, 2)
            ]
            parts = [jnp.concatenate([pair[part] for pair in pairs], 1) for part in range(2)]
        boxed = jnp.concatenate(parts, 0).astype(bf16)
        for first in range(0, groups, 2):
            found = jnp.dot(boxed, hot_ref[:, first * local : (first + 2) * local], preferred_element_type=f32)
            for g in (first, first + 1):
                for part in range(2):
                    total = jnp.zeros((rows, local), f32)
                    for high in range(high_count):
                        start = (part * high_count + high) * rows
                        piece = found[start : start + rows, (g - first) * local : (g - first + 1) * local]
                        total = total + jnp.where(highs[g] == float(high), piece, 0.0)
                    out_ref[g, part * rows : (part + 1) * rows, :] = total.astype(bf16)
        for copy in copies[4:]:
            copy.wait()

    extra = (psi_res,) if bring else ()
    picked, *brought = call_on_chip(
        kernel,
        "apply_planes",
        (received, near),
        (((groups, 2 * rows, local), bf16), *[(array.shape, array.dtype) for array in extra]),
        (*later, *extra),
        (
            *[pltpu.VMEM(array.shape, array.dtype) for array in later],
            pltpu.VMEM((2 * half, sticks), bf16),
            pltpu.VMEM((columns, sticks), bf16),
            pltpu.VMEM((2, box * rows, grid), f32),
            pltpu.VMEM((2, box * rows, grid), f32),
            pltpu.SemaphoreType.DMA((5,)),
        ),
    )
    return picked, brought[0] if bring else psi_res


def image_sticks(sizes, columns, vector, positions):
    depth, local, grid = sizes.depth, sizes.sticks_local, sizes.grid
    height = 2 * depth

    def kernel(table_ref, columns_ref, vector_ref, position_ref, image_ref, rounded_ref, sums_ref):
        product = jnp.dot(table_ref[...], columns_ref[...], preferred_element_type=f32)
        applied = product[:height] + (product[height : 2 * height] + product[2 * height :])
        vector = vector_ref[...]
        x_freq = signed_freq(position_ref[...] // grid, grid)
        y_freq = signed_freq(position_ref[...] % grid, grid)
        row = lax.broadcasted_iota(jnp.int32, (height, local), 0)
        z_freq = jnp.where(row < depth, row, row - depth) - depth // 2
        kinetic = kinetic_unit * (z_freq * z_freq + (x_freq * x_freq + y_freq * y_freq)).astype(f32)
        image = kinetic * vector + applied
        image_ref[...] = image
        rounded_ref[0:height, :] = vector.astype(bf16)
        rounded_ref[height:, :] = image.astype(bf16)
        sums_ref[0:1, :] = jnp.sum(vector * image, axis=0, keepdims=True)
        sums_ref[1:2, :] = jnp.sum(vector * vector, axis=0, keepdims=True)

    return call_on_chip(
        kernel,
        "image_sticks",
        (jnp.asarray(z_forward_table(sizes)), columns, vector, positions),
        (((height, local), f32), ((2 * height, local), bf16), ((2, local), f32)),
    )


def share(product, sums, groups):
    count, width = product.shape
    height = round_up(count + 2, 8)

    def kernel(product_ref, sums_ref, out_ref):
        fill = jnp.zeros((height - count - 2, width), f32)
        partial = jnp.concatenate([product_ref[...], sums_ref[...], fill], 0)
        for group in range(groups):
            out_ref[group] = partial

    return call_on_chip(kernel, "share", (product, sums), (((groups, height, width), f32),))[0]


def finish(copies, image, vector, band, band_total, res_count):
    count = copies.shape[0]
    width = 2 * res_count
    table = np.zeros((width, width), np.float32)
    lane = np.arange(width)
    table[lane, lane % 2 * res_count + lane // 2] = 1.0

    def kernel(band_ref, table_ref, copies_ref, image_ref, vector_ref, residual_ref, ham_ref, inter_ref, total_ref):
        total = copies_ref[0]
        for index in range(1, count):
            total = total + copies_ref[index]
        tail = jnp.sum(total[4 * band_total : 4 * band_total + 2], axis=1, keepdims=True)
        residual_ref[...] = image_ref[...] - (tail[0:1] / tail[1:2]) * vector_ref[...]
        total_ref[...] = jnp.dot(total[: 4 * band_total], table_ref[...], precision=highest, preferred_element_type=f32)
        for column in range(band_total):
            source = column ^ band_ref[0]
            for index, out_ref in enumerate((inter_ref, ham_ref)):
                real = total_ref[pl.ds(source * 4 + index * 2, 1), :]
                imag = total_ref[pl.ds(source * 4 + index * 2 + 1, 1), :]
                out_ref[0, column : column + 1, :] = real[:, :res_count] + imag[:, res_count:]
                out_ref[1, column : column + 1, :] = imag[:, :res_count] - real[:, res_count:]

    spec = pl.BlockSpec(memory_space=pltpu.VMEM)
    operands = (jnp.asarray(table), copies, image, vector)
    projection = jax.ShapeDtypeStruct((2, band_total, res_count), f32)
    return pl.pallas_call(
        kernel,
        out_shape=(jax.ShapeDtypeStruct(image.shape, f32), projection, projection),
        in_specs=[pl.BlockSpec(memory_space=pltpu.SMEM)] + [spec] * 4,
        out_specs=(spec,) * 3,
        scratch_shapes=[pltpu.VMEM((4 * band_total, width), f32)],
        name="finish",
    )(band, *[pltpu.with_memory_space_constraint(operand, pltpu.VMEM) for operand in operands])


def shards(psi_res, correction, local_potential, stick_xy):
    groups, band_total = lax.axis_size("pw"), lax.axis_size("band")
    planes, grid_size = local_potential.shape[:2]
    _, _, stick_depth, sticks_local = correction.shape
    res_count = psi_res.shape[0]
    sizes = Sizes(groups, planes, grid_size, stick_depth, sticks_local)
    potential = jnp.pad(local_potential, ((0, sizes.rows - planes), (0, 0), (0, 0)))
    vector = correction.reshape(2 * stick_depth, sticks_local)

    y_back, x_back, x_forward, y_forward = [jnp.asarray(table) for table in plane_tables(sizes)]
    moving, vector, positions, y_back = spread_sticks(sizes, vector, stick_xy, y_back)
    later = (x_back, potential, x_forward, y_forward)
    moving = lax.all_to_all(moving, "pw", split_axis=0, concat_axis=0, tiled=True)
    picked, psi_near = apply_planes(sizes, moving, y_back, later, psi_res.reshape(2 * res_count, stick_depth, sticks_local))
    picked = lax.all_to_all(picked, "pw", split_axis=0, concat_axis=0, tiled=True)
    picked = picked.reshape(2 * sizes.rows * groups, sticks_local)
    image, rounded, sums = image_sticks(sizes, picked, vector, positions)

    blocks = [rounded] + [
        lax.ppermute(rounded, "band", [(i, i ^ step) for i in range(band_total)]) for step in range(1, band_total)
    ]
    joined = jnp.concatenate(blocks, 0).reshape(4 * band_total, stick_depth, sticks_local)
    product = lax.dot_general(
        joined,
        psi_near,
        (((1, 2), (1, 2)), ((), ())),
        preferred_element_type=f32,
    )
    band = lax.axis_index("band")[None]
    product, band = lax.optimization_barrier((product, band))
    copies = share(product, sums, groups)
    copies = lax.all_to_all(copies, "pw", split_axis=0, concat_axis=0, tiled=True)
    residual, hamiltonian, intersection = finish(copies, image, vector, band, band_total, res_count)
    return (
        residual.reshape(correction.shape),
        jnp.transpose(hamiltonian, (0, 2, 1)),
        jnp.transpose(intersection, (0, 2, 1)),
    )


def solution(mesh):
    return jax.shard_map(
        shards,
        mesh=mesh,
        in_specs=(
            P("band", None, None, "pw"),
            P("band", None, None, "pw"),
            P("pw", None, None),
            P("pw"),
        ),
        out_specs=(P("band", None, None, "pw"), P(None, "band", None), P(None, "band", None)),
        check_vma=False,
    )
```

```python
import math

import jax
import jax.numpy as jnp
import numpy as np
from jax import lax
from jax.experimental import pallas as pl
from jax.experimental.pallas import tpu as pltpu
from jax.sharding import PartitionSpec as P

kinetic_unit = 0.002
highest = lax.Precision.HIGHEST
lanes = 128
f32 = jnp.float32
bf16 = jnp.bfloat16


def round_up(count, step):
    return -(-count // step) * step


def signed_freq(index, grid_size):
    return jnp.where(index < grid_size // 2, index, index - grid_size)


def phases(out_index, in_index, direction, grid_size):
    angles = (out_index[:, None] * in_index[None, :]) % grid_size * (2.0 * math.pi / grid_size)
    cosine, sine = np.cos(angles), direction * np.sin(angles)
    return np.stack([np.stack([cosine, -sine], 1), np.stack([sine, cosine], 1)], 0)


def split(table, count):
    pieces = []
    rest = np.asarray(table, np.float64)
    for _ in range(count):
        piece = rest.astype(jnp.bfloat16)
        pieces.append(piece)
        rest = rest - piece.astype(np.float64)
    return pieces


class Sizes:
    def __init__(self, groups, planes, grid_size, stick_depth, sticks_local):
        self.groups, self.planes = groups, planes
        self.grid, self.depth, self.sticks_local = grid_size, stick_depth, sticks_local
        self.rows = round_up(planes, 16)
        self.sticks = groups * sticks_local
        self.box = round_up(2 * math.ceil(math.sqrt(self.sticks / math.pi)) + 2, 8)
        self.line = round_up(self.box, 64)
        self.low_count = max(1, 256 // self.line)
        self.high_count = self.box // self.low_count


def z_rows(sizes):
    group = np.repeat(np.arange(sizes.groups), sizes.rows)
    plane = np.tile(np.arange(sizes.rows), sizes.groups)
    return group * sizes.planes + plane, plane < sizes.planes


def z_back_table(sizes):
    z_freq = np.arange(sizes.depth) - sizes.depth // 2
    z_index, real = z_rows(sizes)
    table = phases(z_index, z_freq, 1, sizes.grid) * real[None, :, None, None]
    table = table.reshape(2, sizes.groups, sizes.rows, 2 * sizes.depth)
    high, low = split(table.transpose(1, 0, 2, 3).reshape(-1, 2 * sizes.depth), 2)
    return np.concatenate([high, low, high], 1)


def z_forward_table(sizes):
    z_freq = np.arange(sizes.depth) - sizes.depth // 2
    z_index, real = z_rows(sizes)
    table = phases(z_freq, z_index, -1, sizes.grid) * real / float(sizes.grid**3)
    table = table.reshape(2 * sizes.depth, 2, sizes.groups, sizes.rows)
    table = table.transpose(0, 2, 1, 3).reshape(2 * sizes.depth, -1)
    return np.concatenate(split(table, 2), 0)


def plane_tables(sizes):
    grid = np.arange(sizes.grid)
    y_freq = np.arange(sizes.line) - sizes.box // 2
    order = np.arange(sizes.box).reshape(sizes.high_count, sizes.low_count).T.reshape(-1)
    x_freq = order - sizes.box // 2
    inside = np.arange(sizes.line) < sizes.box
    y_back = phases(grid, y_freq, 1, sizes.grid) * inside
    y_back = y_back.reshape(2 * sizes.grid, -1).T
    y_forward = phases(y_freq, grid, -1, sizes.grid) * inside[None, :, None, None]
    y_forward = y_forward.reshape(-1, 2 * sizes.grid).T
    x_back = phases(grid, x_freq, 1, sizes.grid).reshape(2 * sizes.grid, -1)
    x_forward = phases(x_freq, grid, -1, sizes.grid).reshape(-1, 2 * sizes.grid)
    y_back = np.concatenate(split(y_back, 2), 0)
    x_high, x_low = split(x_back, 2)
    x_back = np.concatenate([x_high, x_low, x_high], 1)
    x_forward = np.concatenate(split(x_forward, 2), 0)
    y_forward = np.concatenate(split(y_forward, 2), 1)
    return y_back, x_back, x_forward, y_forward


def call_on_chip(kernel, name, operands, shapes, far=(), scratch=()):
    spec = pl.BlockSpec(memory_space=pltpu.VMEM)
    return pl.pallas_call(
        kernel,
        out_shape=tuple(pltpu.VMEM(shape, dtype) for shape, dtype in shapes),
        in_specs=[spec] * len(operands) + [pl.BlockSpec(memory_space=pl.ANY)] * len(far),
        out_specs=(spec,) * len(shapes),
        scratch_shapes=list(scratch),
        name=name,
    )(*[pltpu.with_memory_space_constraint(operand, pltpu.VMEM) for operand in operands], *far)


def spread_sticks(sizes, vector, positions, others):
    block = 2 * sizes.rows
    z_table = jnp.asarray(z_back_table(sizes))
    kept = (vector, positions[None, :], *others)
    far = (kept[0], z_table, *kept[1:])

    def kernel(*refs):
        distant, (out_ref, *near), (table_ref, sems) = refs[: len(far)], refs[len(far) : -2], refs[-2:]
        vector_ref, position_ref = near[:2]
        copies = [
            pltpu.make_async_copy(source, target, sems.at[index])
            for index, (source, target) in enumerate(zip(distant, (near[0], table_ref, *near[1:]), strict=True))
        ]
        for copy in copies:
            copy.start()
        for copy in copies[:3]:
            copy.wait()
        vector = vector_ref[...]
        high = vector.astype(bf16)
        low = (vector - high.astype(f32)).astype(bf16)
        stacked = jnp.concatenate([high, high, low], 0)
        columns = jnp.dot(table_ref[...], stacked, preferred_element_type=f32)
        x_pos = (position_ref[...] // sizes.grid).astype(f32)
        y_pos = (position_ref[...] % sizes.grid).astype(f32)
        row = lax.broadcasted_iota(jnp.int32, (16, sizes.sticks_local), 0)
        tail = jnp.where(row == 0, x_pos, jnp.where(row == 1, y_pos, 0.0)).astype(bf16)
        for group in range(sizes.groups):
            out_ref[group, 0:block, :] = columns[group * block : (group + 1) * block].astype(bf16)
            out_ref[group, block:, :] = tail
        for copy in copies[3:]:
            copy.wait()

    return call_on_chip(
        kernel,
        "spread_sticks",
        (),
        (((sizes.groups, block + 16, sizes.sticks_local), bf16), *[(array.shape, array.dtype) for array in kept]),
        far,
        [pltpu.VMEM(z_table.shape, z_table.dtype), pltpu.SemaphoreType.DMA((len(far),))],
    )


def turn(position, size):
    angle = (position - 0.5 * size) * (2.0 * math.pi / size)
    square = angle * angle
    cosine = jnp.zeros_like(angle)
    sine = jnp.zeros_like(angle)
    for order in range(7, -1, -1):
        sign = (-1.0) ** order
        cosine = cosine * square + sign / math.factorial(2 * order)
        sine = sine * square + sign / math.factorial(2 * order + 1)
    return -cosine, -sine * angle


def anchor_of(position, grid_size):
    spot = lax.broadcasted_iota(jnp.int32, (1, grid_size), 1).astype(f32)

    def total(values):
        return jnp.sum(jnp.sum(values, axis=0, keepdims=True), axis=1, keepdims=True)

    cosine, sine = turn(position, grid_size)
    spot_cosine, spot_sine = turn(spot, grid_size)
    score = total(cosine) * spot_cosine + total(sine) * spot_sine
    best = jnp.max(score, axis=1, keepdims=True)
    return jnp.min(jnp.where(score >= best, spot, float(grid_size)), axis=1, keepdims=True)


def cross(first, second, line):
    if line % lanes == 0:
        count = first.shape[1] // line
        return [
            jnp.concatenate([side[:, i * line : (i + 1) * line] for side in (first, second)], 1) for i in range(count)
        ]
    low = lax.broadcasted_iota(jnp.int32, (first.shape[0], lanes), 1) < line
    results = []
    for start in range(0, first.shape[1], lanes):
        one, two = first[:, start : start + lanes], second[:, start : start + lanes]
        results.append(jnp.where(low, one, pltpu.roll(two, line, 1)))
        results.append(jnp.where(low, pltpu.roll(one, line, 1), two))
    return results


def apply_planes(sizes, received, near):
    grid, box, line, rows = sizes.grid, sizes.box, sizes.line, sizes.rows
    groups, local, sticks = sizes.groups, sizes.sticks_local, sizes.sticks
    low_count, high_count = sizes.low_count, sizes.high_count
    columns = low_count * line
    half = high_count * rows

    def kernel(in_ref, yb_ref, xb_ref, xf_ref, yf_ref, pot_ref, out_ref, left_ref, hot_ref, a_ref, b_ref):
        def relative(row):
            position = jnp.concatenate([in_ref[g, 2 * rows : 2 * rows + 16, :].astype(f32)[row : row + 1] for g in range(groups)], 0)
            moved = position - anchor_of(position, grid) + float(box // 2)
            moved = jnp.where(moved < 0, moved + float(grid), moved)
            return jnp.where(moved >= float(grid), moved - float(grid), moved)

        x_rel, y_rel = relative(0), relative(1)
        x_high = jnp.floor(x_rel * (1.0 / low_count))
        column = (x_rel - x_high * low_count) * float(line) + y_rel
        step = lax.broadcasted_iota(jnp.int32, (16, local), 0).astype(f32).astype(bf16)
        highs = []
        for g in range(groups):
            where = slice(g * local, (g + 1) * local)
            column_here = jnp.broadcast_to(column[g : g + 1], (16, local)).astype(bf16)
            for start in range(0, columns, 16):
                hot_ref[start : start + 16, where] = jnp.where(
                    column_here == step + jnp.asarray(start, bf16), jnp.asarray(1, bf16), jnp.asarray(0, bf16)
                )
            highs.append(jnp.broadcast_to(x_high[g : g + 1], (rows, local)))
            high_here = highs[g].astype(bf16)
            for part in range(2):
                values = in_ref[g, part * rows : (part + 1) * rows, :]
                for high in range(high_count):
                    start = (part * high_count + high) * rows
                    left_ref[start : start + rows, where] = jnp.where(
                        high_here == jnp.asarray(high, bf16), values, jnp.asarray(0, bf16)
                    )

        placed = lax.dot_general(left_ref[...], hot_ref[...], (((1,), (1,)), ((), ())), preferred_element_type=f32)
        placed = jnp.concatenate(cross(placed[:half], placed[half:], line), 0).astype(bf16)
        lines = jnp.dot(jnp.concatenate([placed, placed], 1), yb_ref[...], preferred_element_type=f32)
        for part in range(2):
            a_ref[part] = lines[:, part * grid : (part + 1) * grid]

        def to_field(first):
            high, low = [], []
            for plane in (first, first + 1):
                lines = jnp.concatenate([a_ref[part, pl.ds(plane, box, stride=rows), :] for part in range(2)], 0)
                high.append(lines.astype(bf16))
                low.append((lines - high[-1].astype(f32)).astype(bf16))
            high, low = jnp.concatenate(high, 1), jnp.concatenate(low, 1)
            field = jnp.dot(xb_ref[...], jnp.concatenate([high, high, low], 0), preferred_element_type=f32)
            weight = jnp.concatenate([pot_ref[first], pot_ref[first + 1]], 1)
            return (field * jnp.concatenate([weight, weight], 0)).astype(bf16)

        def from_field(first, field):
            back = jnp.dot(xf_ref[...], field, preferred_element_type=f32)
            back = back[: 2 * box] + back[2 * box :]
            for index in range(2):
                for part in range(2):
                    b_ref[part, pl.ds(first + index, box, stride=rows), :] = back[
                        part * box : (part + 1) * box, index * grid : (index + 1) * grid
                    ]

        fields = [to_field(0)]
        for first in range(0, rows, 2):
            if first + 2 < rows:
                fields.append(to_field(first + 2))
            from_field(first, fields[first // 2])

        lines = jnp.concatenate([b_ref[0], b_ref[1]], 1).astype(bf16)
        boxed = jnp.dot(lines, yf_ref[...], preferred_element_type=f32)
        boxed = boxed[:, : 2 * line] + boxed[:, 2 * line :]
        if line % lanes == 0:
            parts = [
                jnp.concatenate([boxed[low * half : (low + 1) * half, part * line : (part + 1) * line] for low in range(low_count)], 1)
                for part in range(2)
            ]
        else:
            pairs = [
                cross(boxed[low * half : (low + 1) * half], boxed[(low + 1) * half : (low + 2) * half], line)
                for low in range(0, low_count, 2)
            ]
            parts = [jnp.concatenate([pair[part] for pair in pairs], 1) for part in range(2)]
        boxed = jnp.concatenate(parts, 0).astype(bf16)
        for first in range(0, groups, 2):
            found = jnp.dot(boxed, hot_ref[:, first * local : (first + 2) * local], preferred_element_type=f32)
            for g in (first, first + 1):
                for part in range(2):
                    total = jnp.zeros((rows, local), f32)
                    for high in range(high_count):
                        start = (part * high_count + high) * rows
                        piece = found[start : start + rows, (g - first) * local : (g - first + 1) * local]
                        total = total + jnp.where(highs[g] == float(high), piece, 0.0)
                    out_ref[g, part * rows : (part + 1) * rows, :] = total.astype(bf16)

    return call_on_chip(
        kernel,
        "apply_planes",
        (received, *near),
        (((groups, 2 * rows, local), bf16),),
        scratch=(
            pltpu.VMEM((2 * half, sticks), bf16),
            pltpu.VMEM((columns, sticks), bf16),
            pltpu.VMEM((2, box * rows, grid), f32),
            pltpu.VMEM((2, box * rows, grid), f32),
        ),
    )[0]


def image_sticks(sizes, columns, vector, positions):
    depth, local, grid = sizes.depth, sizes.sticks_local, sizes.grid
    height = 2 * depth

    def kernel(table_ref, columns_ref, vector_ref, position_ref, image_ref, rounded_ref, sums_ref):
        product = jnp.dot(table_ref[...], columns_ref[...], preferred_element_type=f32)
        applied = product[:height] + product[height:]
        vector = vector_ref[...]
        x_freq = signed_freq(position_ref[...] // grid, grid)
        y_freq = signed_freq(position_ref[...] % grid, grid)
        row = lax.broadcasted_iota(jnp.int32, (height, local), 0)
        z_freq = jnp.where(row < depth, row, row - depth) - depth // 2
        kinetic = kinetic_unit * (z_freq * z_freq + (x_freq * x_freq + y_freq * y_freq)).astype(f32)
        image = kinetic * vector + applied
        image_ref[...] = image
        rounded_ref[0:height, :] = vector.astype(bf16)
        rounded_ref[height:, :] = image.astype(bf16)
        sums_ref[0:1, :] = jnp.sum(vector * image, axis=0, keepdims=True)
        sums_ref[1:2, :] = jnp.sum(vector * vector, axis=0, keepdims=True)

    return call_on_chip(
        kernel,
        "image_sticks",
        (jnp.asarray(z_forward_table(sizes)), columns, vector, positions),
        (((height, local), f32), ((2 * height, local), bf16), ((2, local), f32)),
    )


def bring(array, after):
    def kernel(after_ref, far_ref, out_ref, sem):
        copy = pltpu.make_async_copy(far_ref, out_ref, sem)
        copy.start()
        copy.wait()

    return call_on_chip(
        kernel, "bring", (after,), ((array.shape, array.dtype),), (array,), (pltpu.SemaphoreType.DMA(()),)
    )[0]


def share(product, sums, groups):
    count, width = product.shape
    height = round_up(count + 2, 8)

    def kernel(product_ref, sums_ref, out_ref):
        fill = jnp.zeros((height - count - 2, width), f32)
        partial = jnp.concatenate([product_ref[...], sums_ref[...], fill], 0)
        for group in range(groups):
            out_ref[group] = partial

    return call_on_chip(kernel, "share", (product, sums), (((groups, height, width), f32),))[0]


def finish(copies, image, vector, band, band_total, res_count):
    count = copies.shape[0]
    width = 2 * res_count

    def kernel(band_ref, copies_ref, image_ref, vector_ref, residual_ref, ham_ref, inter_ref, total_ref):
        total = copies_ref[0]
        for index in range(1, count):
            total = total + copies_ref[index]
        tail = jnp.sum(total[4 * band_total : 4 * band_total + 2], axis=1, keepdims=True)
        residual_ref[...] = image_ref[...] - (tail[0:1] / tail[1:2]) * vector_ref[...]
        source = lax.broadcasted_iota(jnp.int32, (width, width), 0)
        target = lax.broadcasted_iota(jnp.int32, (width, width), 1)
        table = jnp.where(target == source % 2 * res_count + source // 2, 1.0, 0.0)
        total_ref[...] = jnp.dot(total[: 4 * band_total], table, precision=highest, preferred_element_type=f32)
        for column in range(band_total):
            source = column ^ band_ref[0]
            for index, out_ref in enumerate((inter_ref, ham_ref)):
                real = total_ref[pl.ds(source * 4 + index * 2, 1), :]
                imag = total_ref[pl.ds(source * 4 + index * 2 + 1, 1), :]
                out_ref[0, column : column + 1, :] = real[:, :res_count] + imag[:, res_count:]
                out_ref[1, column : column + 1, :] = imag[:, :res_count] - real[:, res_count:]

    spec = pl.BlockSpec(memory_space=pltpu.VMEM)
    operands = (copies, image, vector)
    projection = jax.ShapeDtypeStruct((2, band_total, res_count), f32)
    return pl.pallas_call(
        kernel,
        out_shape=(jax.ShapeDtypeStruct(image.shape, f32), projection, projection),
        in_specs=[pl.BlockSpec(memory_space=pltpu.SMEM)] + [spec] * 3,
        out_specs=(spec,) * 3,
        scratch_shapes=[pltpu.VMEM((4 * band_total, width), f32)],
        name="finish",
    )(band, *[pltpu.with_memory_space_constraint(operand, pltpu.VMEM) for operand in operands])


def shards(psi_res, correction, local_potential, stick_xy):
    groups, band_total = lax.axis_size("pw"), lax.axis_size("band")
    planes, grid_size = local_potential.shape[:2]
    _, _, stick_depth, sticks_local = correction.shape
    res_count = psi_res.shape[0]
    sizes = Sizes(groups, planes, grid_size, stick_depth, sticks_local)
    potential = jnp.pad(local_potential, ((0, sizes.rows - planes), (0, 0), (0, 0)))
    vector = correction.reshape(2 * stick_depth, sticks_local)

    others = [*[jnp.asarray(table) for table in plane_tables(sizes)], potential]
    moving, vector, positions, *near = spread_sticks(sizes, vector, stick_xy, others)
    moving = lax.all_to_all(moving, "pw", split_axis=0, concat_axis=0, tiled=True)
    picked = apply_planes(sizes, moving, near)
    picked = lax.all_to_all(picked, "pw", split_axis=0, concat_axis=0, tiled=True)
    picked = picked.reshape(2 * sizes.rows * groups, sticks_local)
    image, rounded, sums = image_sticks(sizes, picked, vector, positions)

    blocks = [rounded] + [
        lax.ppermute(rounded, "band", [(i, i ^ step) for i in range(band_total)]) for step in range(1, band_total)
    ]
    psi_near = bring(psi_res.reshape(2 * res_count, stick_depth, sticks_local), sums)
    joined = jnp.concatenate(blocks, 0).reshape(4 * band_total, stick_depth, sticks_local)
    product = lax.dot_general(
        joined,
        psi_near,
        (((1, 2), (1, 2)), ((), ())),
        preferred_element_type=f32,
    )
    band = lax.axis_index("band")[None]
    product, band = lax.optimization_barrier((product, band))
    copies = share(product, sums, groups)
    copies = lax.all_to_all(copies, "pw", split_axis=0, concat_axis=0, tiled=True)
    residual, hamiltonian, intersection = finish(copies, image, vector, band, band_total, res_count)
    return (
        residual.reshape(correction.shape),
        jnp.transpose(hamiltonian, (0, 2, 1)),
        jnp.transpose(intersection, (0, 2, 1)),
    )


def solution(mesh):
    return jax.shard_map(
        shards,
        mesh=mesh,
        in_specs=(
            P("band", None, None, "pw"),
            P("band", None, None, "pw"),
            P("pw", None, None),
            P("pw"),
        ),
        out_specs=(P("band", None, None, "pw"), P(None, "band", None), P(None, "band", None)),
        check_vma=False,
    )
```

```python
import math

import jax
import jax.numpy as jnp
import numpy as np
from jax import lax
from jax.experimental import pallas as pl
from jax.experimental.pallas import tpu as pltpu
from jax.sharding import PartitionSpec as P

kinetic_unit = 0.002
highest = lax.Precision.HIGHEST
lanes = 128
f32 = jnp.float32
bf16 = jnp.bfloat16


def round_up(count, step):
    return -(-count // step) * step


def signed_freq(index, grid_size):
    return jnp.where(index < grid_size // 2, index, index - grid_size)


def phases(out_index, in_index, direction, grid_size):
    angles = (out_index[:, None] * in_index[None, :]) % grid_size * (2.0 * math.pi / grid_size)
    cosine, sine = np.cos(angles), direction * np.sin(angles)
    return np.stack([np.stack([cosine, -sine], 1), np.stack([sine, cosine], 1)], 0)


def split(table, count):
    pot_copy = []
    rest = np.asarray(table, np.float64)
    for _ in range(count):
        piece = rest.astype(jnp.bfloat16)
        pot_copy.append(piece)
        rest = rest - piece.astype(np.float64)
    return pot_copy


class Sizes:
    def __init__(self, groups, planes, grid_size, stick_depth, sticks_local):
        self.groups, self.planes = groups, planes
        self.grid, self.depth, self.sticks_local = grid_size, stick_depth, sticks_local
        self.rows = round_up(planes, 16)
        self.sticks = groups * sticks_local
        self.box = round_up(2 * math.ceil(math.sqrt(self.sticks / math.pi)) + 2, 8)
        self.line = round_up(self.box, 64)
        self.low_count = max(1, 256 // self.line)
        self.high_count = self.box // self.low_count


def z_rows(sizes):
    group = np.repeat(np.arange(sizes.groups), sizes.rows)
    plane = np.tile(np.arange(sizes.rows), sizes.groups)
    return group * sizes.planes + plane, plane < sizes.planes


def z_back_table(sizes):
    z_freq = np.arange(sizes.depth) - sizes.depth // 2
    z_index, real = z_rows(sizes)
    table = phases(z_index, z_freq, 1, sizes.grid) * real[None, :, None, None]
    table = table.reshape(2, sizes.groups, sizes.rows, 2 * sizes.depth)
    high, low = split(table.transpose(1, 0, 2, 3).reshape(-1, 2 * sizes.depth), 2)
    return np.concatenate([high, low, high], 1)


def z_forward_table(sizes):
    z_freq = np.arange(sizes.depth) - sizes.depth // 2
    z_index, real = z_rows(sizes)
    table = phases(z_freq, z_index, -1, sizes.grid) * real / float(sizes.grid**3)
    table = table.reshape(2 * sizes.depth, 2, sizes.groups, sizes.rows)
    table = table.transpose(0, 2, 1, 3).reshape(2 * sizes.depth, -1)
    return np.concatenate(split(table, 2), 0)


def plane_tables(sizes):
    grid = np.arange(sizes.grid)
    y_freq = np.arange(sizes.line) - sizes.box // 2
    order = np.arange(sizes.box).reshape(sizes.high_count, sizes.low_count).T.reshape(-1)
    x_freq = order - sizes.box // 2
    inside = np.arange(sizes.line) < sizes.box
    y_back = phases(grid, y_freq, 1, sizes.grid) * inside
    y_back = y_back.reshape(2 * sizes.grid, -1).T
    y_forward = phases(y_freq, grid, -1, sizes.grid) * inside[None, :, None, None]
    y_forward = y_forward.reshape(-1, 2 * sizes.grid).T
    x_back = phases(grid, x_freq, 1, sizes.grid).reshape(2 * sizes.grid, -1)
    x_forward = phases(x_freq, grid, -1, sizes.grid).reshape(-1, 2 * sizes.grid)
    y_back = np.concatenate(split(y_back, 2), 0)
    x_high, x_low = split(x_back, 2)
    x_back = np.concatenate([x_high, x_low, x_high], 1)
    x_forward = np.concatenate(split(x_forward, 2), 0)
    y_forward = np.concatenate(split(y_forward, 2), 1)
    return y_back, x_back, x_forward, y_forward


def call_on_chip(kernel, name, operands, shapes, far=(), scratch=()):
    spec = pl.BlockSpec(memory_space=pltpu.VMEM)
    return pl.pallas_call(
        kernel,
        out_shape=tuple(pltpu.VMEM(shape, dtype) for shape, dtype in shapes),
        in_specs=[spec] * len(operands) + [pl.BlockSpec(memory_space=pl.ANY)] * len(far),
        out_specs=(spec,) * len(shapes),
        scratch_shapes=list(scratch),
        name=name,
    )(*[pltpu.with_memory_space_constraint(operand, pltpu.VMEM) for operand in operands], *far)


def spread_sticks(sizes, vector, positions, y_back):
    block = 2 * sizes.rows
    z_table = jnp.asarray(z_back_table(sizes))
    kept = (vector, positions[None, :], y_back)
    far = (kept[0], z_table, *kept[1:])

    def kernel(*refs):
        distant, (out_ref, *near), (table_ref, sems) = refs[: len(far)], refs[len(far) : -2], refs[-2:]
        vector_ref, position_ref = near[:2]
        copies = [
            pltpu.make_async_copy(source, target, sems.at[index])
            for index, (source, target) in enumerate(zip(distant, (near[0], table_ref, *near[1:]), strict=True))
        ]
        for copy in copies:
            copy.start()
        for copy in copies[:3]:
            copy.wait()
        vector = vector_ref[...]
        high = vector.astype(bf16)
        low = (vector - high.astype(f32)).astype(bf16)
        stacked = jnp.concatenate([high, high, low], 0)
        columns = jnp.dot(table_ref[...], stacked, preferred_element_type=f32)
        x_pos = (position_ref[...] // sizes.grid).astype(f32)
        y_pos = (position_ref[...] % sizes.grid).astype(f32)
        row = lax.broadcasted_iota(jnp.int32, (16, sizes.sticks_local), 0)
        tail = jnp.where(row == 0, x_pos, jnp.where(row == 1, y_pos, 0.0)).astype(bf16)
        for group in range(sizes.groups):
            out_ref[group, 0:block, :] = columns[group * block : (group + 1) * block].astype(bf16)
            out_ref[group, block:, :] = tail
        for copy in copies[3:]:
            copy.wait()

    return call_on_chip(
        kernel,
        "spread_sticks",
        (),
        (((sizes.groups, block + 16, sizes.sticks_local), bf16), *[(array.shape, array.dtype) for array in kept]),
        far,
        [pltpu.VMEM(z_table.shape, z_table.dtype), pltpu.SemaphoreType.DMA((len(far),))],
    )


def turn(position, size):
    angle = (position - 0.5 * size) * (2.0 * math.pi / size)
    square = angle * angle
    cosine = jnp.zeros_like(angle)
    sine = jnp.zeros_like(angle)
    for order in range(7, -1, -1):
        sign = (-1.0) ** order
        cosine = cosine * square + sign / math.factorial(2 * order)
        sine = sine * square + sign / math.factorial(2 * order + 1)
    return -cosine, -sine * angle


def anchor_of(position, grid_size):
    spot = lax.broadcasted_iota(jnp.int32, (1, grid_size), 1).astype(f32)

    def total(values):
        return jnp.sum(jnp.sum(values, axis=0, keepdims=True), axis=1, keepdims=True)

    cosine, sine = turn(position, grid_size)
    spot_cosine, spot_sine = turn(spot, grid_size)
    score = total(cosine) * spot_cosine + total(sine) * spot_sine
    best = jnp.max(score, axis=1, keepdims=True)
    return jnp.min(jnp.where(score >= best, spot, float(grid_size)), axis=1, keepdims=True)


def cross(first, second, line):
    if line % lanes == 0:
        count = first.shape[1] // line
        return [
            jnp.concatenate([side[:, i * line : (i + 1) * line] for side in (first, second)], 1) for i in range(count)
        ]
    low = lax.broadcasted_iota(jnp.int32, (first.shape[0], lanes), 1) < line
    results = []
    for start in range(0, first.shape[1], lanes):
        one, two = first[:, start : start + lanes], second[:, start : start + lanes]
        results.append(jnp.where(low, one, pltpu.roll(two, line, 1)))
        results.append(jnp.where(low, pltpu.roll(one, line, 1), two))
    return results


def apply_planes(sizes, received, near, later, psi_res):
    grid, box, line, rows = sizes.grid, sizes.box, sizes.line, sizes.rows
    groups, local, sticks = sizes.groups, sizes.sticks_local, sizes.sticks
    low_count, high_count = sizes.low_count, sizes.high_count
    columns = low_count * line
    half = high_count * rows

    psi_bytes, other_bytes = (sum(array.nbytes for array in arrays) for arrays in ((psi_res,), (received, received, near)))
    fits = psi_bytes + other_bytes < 3200000

    def kernel(in_ref, yb_ref, *refs):
        *distant, out_ref = refs[:5]
        scratch = refs[5:]
        if fits:
            *distant, psi_far = refs[:5]
            out_ref, psi_ref, *scratch = refs[5:]
            psi_copy = pltpu.make_async_copy(psi_far, psi_ref, scratch[-1].at[4])
        *near_refs, left_ref, hot_ref, a_ref, b_ref, field_ref, sems = scratch
        xb_ref, pot_ref, xf_ref, yf_ref = near_refs
        tables = [
            pltpu.make_async_copy(distant[index], near_refs[index], sems.at[slot])
            for slot, index in enumerate((0, 2, 3))
        ]
        pot_copy = pltpu.make_async_copy(distant[1], pot_ref, sems.at[3])
        for copy in (tables[0], pot_copy, *tables[1:]):
            copy.start()
        if fits:
            psi_copy.start()

        def relative(row):
            position = jnp.concatenate([in_ref[g, 2 * rows : 2 * rows + 16, :].astype(f32)[row : row + 1] for g in range(groups)], 0)
            moved = position - anchor_of(position, grid) + float(box // 2)
            moved = jnp.where(moved < 0, moved + float(grid), moved)
            return jnp.where(moved >= float(grid), moved - float(grid), moved)

        x_rel, y_rel = relative(0), relative(1)
        x_high = jnp.floor(x_rel * (1.0 / low_count))
        column = (x_rel - x_high * low_count) * float(line) + y_rel
        step = lax.broadcasted_iota(jnp.int32, (16, local), 0).astype(f32).astype(bf16)
        highs = []
        for g in range(groups):
            where = slice(g * local, (g + 1) * local)
            column_here = jnp.broadcast_to(column[g : g + 1], (16, local)).astype(bf16)
            for start in range(0, columns, 16):
                hot_ref[start : start + 16, where] = jnp.where(
                    column_here == step + jnp.asarray(start, bf16), jnp.asarray(1, bf16), jnp.asarray(0, bf16)
                )
            highs.append(jnp.broadcast_to(x_high[g : g + 1], (rows, local)))
            high_here = highs[g].astype(bf16)
            for part in range(2):
                values = in_ref[g, part * rows : (part + 1) * rows, :]
                for high in range(high_count):
                    start = (part * high_count + high) * rows
                    left_ref[start : start + rows, where] = jnp.where(
                        high_here == jnp.asarray(high, bf16), values, jnp.asarray(0, bf16)
                    )

        placed = lax.dot_general(left_ref[...], hot_ref[...], (((1,), (1,)), ((), ())), preferred_element_type=f32)
        placed = jnp.concatenate(cross(placed[:half], placed[half:], line), 0).astype(bf16)
        lines = jnp.dot(jnp.concatenate([placed, placed], 1), yb_ref[...], preferred_element_type=f32)
        for part in range(2):
            a_ref[part] = lines[:, part * grid : (part + 1) * grid]

        tables[0].wait()
        for first in range(0, rows, 2):
            high, low = [], []
            for plane in (first, first + 1):
                lines = jnp.concatenate([a_ref[part, pl.ds(plane, box, stride=rows), :] for part in range(2)], 0)
                high.append(lines.astype(bf16))
                low.append((lines - high[-1].astype(f32)).astype(bf16))
            high, low = jnp.concatenate(high, 1), jnp.concatenate(low, 1)
            field_ref[first // 2] = jnp.dot(xb_ref[...], jnp.concatenate([high, high, low], 0), preferred_element_type=f32)
        for copy in (pot_copy, tables[1], tables[2]):
            copy.wait()
        for first in range(0, rows, 2):
            weight = jnp.concatenate([pot_ref[first], pot_ref[first + 1]], 1)
            field = (field_ref[first // 2] * jnp.concatenate([weight, weight], 0)).astype(bf16)
            back = jnp.dot(xf_ref[...], field, preferred_element_type=f32)
            back = back[: 2 * box] + back[2 * box :]
            for index in range(2):
                for part in range(2):
                    b_ref[part, pl.ds(first + index, box, stride=rows), :] = back[
                        part * box : (part + 1) * box, index * grid : (index + 1) * grid
                    ]

        lines = jnp.concatenate([b_ref[0], b_ref[1]], 1).astype(bf16)
        boxed = jnp.dot(lines, yf_ref[...], preferred_element_type=f32)
        boxed = boxed[:, : 2 * line] + boxed[:, 2 * line :]
        if line % lanes == 0:
            parts = [
                jnp.concatenate([boxed[low * half : (low + 1) * half, part * line : (part + 1) * line] for low in range(low_count)], 1)
                for part in range(2)
            ]
        else:
            pairs = [
                cross(boxed[low * half : (low + 1) * half], boxed[(low + 1) * half : (low + 2) * half], line)
                for low in range(0, low_count, 2)
            ]
            parts = [jnp.concatenate([pair[part] for pair in pairs], 1) for part in range(2)]
        boxed = jnp.concatenate(parts, 0).astype(bf16)
        for first in range(0, groups, 2):
            found = jnp.dot(boxed, hot_ref[:, first * local : (first + 2) * local], preferred_element_type=f32)
            for g in (first, first + 1):
                for part in range(2):
                    total = jnp.zeros((rows, local), f32)
                    for high in range(high_count):
                        start = (part * high_count + high) * rows
                        piece = found[start : start + rows, (g - first) * local : (g - first + 1) * local]
                        total = total + jnp.where(highs[g] == float(high), piece, 0.0)
                    out_ref[g, part * rows : (part + 1) * rows, :] = total.astype(bf16)
        if fits:
            psi_copy.wait()

    extra = (psi_res,) if fits else ()
    picked, *brought = call_on_chip(
        kernel,
        "apply_planes",
        (received, near),
        (((groups, 2 * rows, local), bf16), *[(array.shape, array.dtype) for array in extra]),
        (*later, *extra),
        (
            *[pltpu.VMEM(array.shape, array.dtype) for array in later],
            pltpu.VMEM((2 * half, sticks), bf16),
            pltpu.VMEM((columns, sticks), bf16),
            pltpu.VMEM((2, box * rows, grid), f32),
            pltpu.VMEM((2, box * rows, grid), f32),
            pltpu.VMEM((rows // 2, 2 * grid, 2 * grid), f32),
            pltpu.SemaphoreType.DMA((5,)),
        ),
    )
    return picked, brought[0] if fits else psi_res


def image_sticks(sizes, columns, vector, positions):
    depth, local, grid = sizes.depth, sizes.sticks_local, sizes.grid
    height = 2 * depth

    def kernel(table_ref, columns_ref, vector_ref, position_ref, image_ref, rounded_ref, sums_ref):
        product = jnp.dot(table_ref[...], columns_ref[...], preferred_element_type=f32)
        applied = product[:height] + product[height:]
        vector = vector_ref[...]
        x_freq = signed_freq(position_ref[...] // grid, grid)
        y_freq = signed_freq(position_ref[...] % grid, grid)
        row = lax.broadcasted_iota(jnp.int32, (height, local), 0)
        z_freq = jnp.where(row < depth, row, row - depth) - depth // 2
        kinetic = kinetic_unit * (z_freq * z_freq + (x_freq * x_freq + y_freq * y_freq)).astype(f32)
        image = kinetic * vector + applied
        image_ref[...] = image
        rounded_ref[0:height, :] = vector.astype(bf16)
        rounded_ref[height:, :] = image.astype(bf16)
        sums_ref[0:1, :] = jnp.sum(vector * image, axis=0, keepdims=True)
        sums_ref[1:2, :] = jnp.sum(vector * vector, axis=0, keepdims=True)

    return call_on_chip(
        kernel,
        "image_sticks",
        (jnp.asarray(z_forward_table(sizes)), columns, vector, positions),
        (((height, local), f32), ((2 * height, local), bf16), ((2, local), f32)),
    )


def share(product, sums, groups):
    count, width = product.shape
    height = round_up(count + 2, 8)

    def kernel(product_ref, sums_ref, out_ref):
        fill = jnp.zeros((height - count - 2, width), f32)
        partial = jnp.concatenate([product_ref[...], sums_ref[...], fill], 0)
        for group in range(groups):
            out_ref[group] = partial

    return call_on_chip(kernel, "share", (product, sums), (((groups, height, width), f32),))[0]


def finish(copies, image, vector, band, band_total, res_count):
    count = copies.shape[0]
    width = 2 * res_count

    def kernel(band_ref, copies_ref, image_ref, vector_ref, residual_ref, ham_ref, inter_ref, total_ref):
        total = copies_ref[0]
        for index in range(1, count):
            total = total + copies_ref[index]
        tail = jnp.sum(total[4 * band_total : 4 * band_total + 2], axis=1, keepdims=True)
        residual_ref[...] = image_ref[...] - (tail[0:1] / tail[1:2]) * vector_ref[...]
        source = lax.broadcasted_iota(jnp.int32, (width, width), 0)
        target = lax.broadcasted_iota(jnp.int32, (width, width), 1)
        table = jnp.where(target == source % 2 * res_count + source // 2, 1.0, 0.0)
        total_ref[...] = jnp.dot(total[: 4 * band_total], table, precision=highest, preferred_element_type=f32)
        for column in range(band_total):
            source = column ^ band_ref[0]
            for index, out_ref in enumerate((inter_ref, ham_ref)):
                real = total_ref[pl.ds(source * 4 + index * 2, 1), :]
                imag = total_ref[pl.ds(source * 4 + index * 2 + 1, 1), :]
                out_ref[0, column : column + 1, :] = real[:, :res_count] + imag[:, res_count:]
                out_ref[1, column : column + 1, :] = imag[:, :res_count] - real[:, res_count:]

    spec = pl.BlockSpec(memory_space=pltpu.VMEM)
    operands = (copies, image, vector)
    projection = jax.ShapeDtypeStruct((2, band_total, res_count), f32)
    return pl.pallas_call(
        kernel,
        out_shape=(jax.ShapeDtypeStruct(image.shape, f32), projection, projection),
        in_specs=[pl.BlockSpec(memory_space=pltpu.SMEM)] + [spec] * 3,
        out_specs=(spec,) * 3,
        scratch_shapes=[pltpu.VMEM((4 * band_total, width), f32)],
        name="finish",
    )(band, *[pltpu.with_memory_space_constraint(operand, pltpu.VMEM) for operand in operands])


def shards(psi_res, correction, local_potential, stick_xy):
    groups, band_total = lax.axis_size("pw"), lax.axis_size("band")
    planes, grid_size = local_potential.shape[:2]
    _, _, stick_depth, sticks_local = correction.shape
    res_count = psi_res.shape[0]
    sizes = Sizes(groups, planes, grid_size, stick_depth, sticks_local)
    potential = jnp.pad(local_potential, ((0, sizes.rows - planes), (0, 0), (0, 0)))
    vector = correction.reshape(2 * stick_depth, sticks_local)

    y_back, x_back, x_forward, y_forward = [jnp.asarray(table) for table in plane_tables(sizes)]
    moving, vector, positions, y_back = spread_sticks(sizes, vector, stick_xy, y_back)
    later = (x_back, potential, x_forward, y_forward)
    moving = lax.all_to_all(moving, "pw", split_axis=0, concat_axis=0, tiled=True)
    picked, psi_near = apply_planes(sizes, moving, y_back, later, psi_res.reshape(2 * res_count, stick_depth, sticks_local))
    picked = lax.all_to_all(picked, "pw", split_axis=0, concat_axis=0, tiled=True)
    picked = picked.reshape(2 * sizes.rows * groups, sticks_local)
    image, rounded, sums = image_sticks(sizes, picked, vector, positions)

    blocks = [rounded] + [
        lax.ppermute(rounded, "band", [(i, i ^ step) for i in range(band_total)]) for step in range(1, band_total)
    ]
    joined = jnp.concatenate(blocks, 0).reshape(4 * band_total, stick_depth, sticks_local)
    product = lax.dot_general(
        joined,
        psi_near,
        (((1, 2), (1, 2)), ((), ())),
        preferred_element_type=f32,
    )
    band = lax.axis_index("band")[None]
    product, band = lax.optimization_barrier((product, band))
    copies = share(product, sums, groups)
    copies = lax.all_to_all(copies, "pw", split_axis=0, concat_axis=0, tiled=True)
    residual, hamiltonian, intersection = finish(copies, image, vector, band, band_total, res_count)
    return (
        residual.reshape(correction.shape),
        jnp.transpose(hamiltonian, (0, 2, 1)),
        jnp.transpose(intersection, (0, 2, 1)),
    )


def solution(mesh):
    return jax.shard_map(
        shards,
        mesh=mesh,
        in_specs=(
            P("band", None, None, "pw"),
            P("band", None, None, "pw"),
            P("pw", None, None),
            P("pw"),
        ),
        out_specs=(P("band", None, None, "pw"), P(None, "band", None), P(None, "band", None)),
        check_vma=False,
    )
```

```python
import math

import jax
import jax.numpy as jnp
import numpy as np
from jax import lax
from jax.experimental import pallas as pl
from jax.experimental.pallas import tpu as pltpu
from jax.sharding import PartitionSpec as P

kinetic_unit = 0.002
highest = lax.Precision.HIGHEST
lanes = 128
f32 = jnp.float32
bf16 = jnp.bfloat16


def round_up(count, step):
    return -(-count // step) * step


def signed_freq(index, grid_size):
    return jnp.where(index < grid_size // 2, index, index - grid_size)


def phases(out_index, in_index, direction, grid_size):
    angles = (out_index[:, None] * in_index[None, :]) % grid_size * (2.0 * math.pi / grid_size)
    cosine, sine = np.cos(angles), direction * np.sin(angles)
    return np.stack([np.stack([cosine, -sine], 1), np.stack([sine, cosine], 1)], 0)


def split(table, count):
    pot_copy = []
    rest = np.asarray(table, np.float64)
    for _ in range(count):
        piece = rest.astype(jnp.bfloat16)
        pot_copy.append(piece)
        rest = rest - piece.astype(np.float64)
    return pot_copy


class Sizes:
    def __init__(self, groups, planes, grid_size, stick_depth, sticks_local):
        self.groups, self.planes = groups, planes
        self.grid, self.depth, self.sticks_local = grid_size, stick_depth, sticks_local
        self.rows = round_up(planes, 16)
        self.sticks = groups * sticks_local
        self.box = round_up(2 * math.ceil(math.sqrt(self.sticks / math.pi)) + 2, 8)
        self.line = round_up(self.box, 64)
        self.low_count = max(1, 256 // self.line)
        self.high_count = self.box // self.low_count


def z_rows(sizes):
    group = np.repeat(np.arange(sizes.groups), sizes.rows)
    plane = np.tile(np.arange(sizes.rows), sizes.groups)
    return group * sizes.planes + plane, plane < sizes.planes


def z_back_table(sizes):
    z_freq = np.arange(sizes.depth) - sizes.depth // 2
    z_index, real = z_rows(sizes)
    table = phases(z_index, z_freq, 1, sizes.grid) * real[None, :, None, None]
    table = table.reshape(2, sizes.groups, sizes.rows, 2 * sizes.depth)
    high, low = split(table.transpose(1, 0, 2, 3).reshape(-1, 2 * sizes.depth), 2)
    return np.concatenate([high, low, high], 1)


def z_forward_table(sizes):
    z_freq = np.arange(sizes.depth) - sizes.depth // 2
    z_index, real = z_rows(sizes)
    table = phases(z_freq, z_index, -1, sizes.grid) * real / float(sizes.grid**3)
    table = table.reshape(2 * sizes.depth, 2, sizes.groups, sizes.rows)
    table = table.transpose(0, 2, 1, 3).reshape(2 * sizes.depth, -1)
    return np.concatenate(split(table, 2), 0)


def plane_tables(sizes):
    grid = np.arange(sizes.grid)
    y_freq = np.arange(sizes.line) - sizes.box // 2
    order = np.arange(sizes.box).reshape(sizes.high_count, sizes.low_count).T.reshape(-1)
    x_freq = order - sizes.box // 2
    inside = np.arange(sizes.line) < sizes.box
    y_back = phases(grid, y_freq, 1, sizes.grid) * inside
    y_back = y_back.reshape(2 * sizes.grid, -1).T
    y_forward = phases(y_freq, grid, -1, sizes.grid) * inside[None, :, None, None]
    y_forward = y_forward.reshape(-1, 2 * sizes.grid).T
    x_back = phases(grid, x_freq, 1, sizes.grid).reshape(2 * sizes.grid, -1)
    x_forward = phases(x_freq, grid, -1, sizes.grid).reshape(-1, 2 * sizes.grid)
    y_back = np.concatenate(split(y_back, 2), 0)
    x_high, x_low = split(x_back, 2)
    x_back = np.concatenate([x_high, x_low, x_high], 1)
    x_forward = np.concatenate(split(x_forward, 2), 0)
    y_forward = np.concatenate(split(y_forward, 2), 1)
    return y_back, x_back, x_forward, y_forward


def call_on_chip(kernel, name, operands, shapes, far=(), scratch=()):
    spec = pl.BlockSpec(memory_space=pltpu.VMEM)
    return pl.pallas_call(
        kernel,
        out_shape=tuple(pltpu.VMEM(shape, dtype) for shape, dtype in shapes),
        in_specs=[spec] * len(operands) + [pl.BlockSpec(memory_space=pl.ANY)] * len(far),
        out_specs=(spec,) * len(shapes),
        scratch_shapes=list(scratch),
        name=name,
    )(*[pltpu.with_memory_space_constraint(operand, pltpu.VMEM) for operand in operands], *far)


def spread_sticks(sizes, vector, positions, y_back):
    block = 2 * sizes.rows
    z_table = jnp.asarray(z_back_table(sizes))
    kept = (vector, positions[None, :], y_back)
    far = (kept[0], z_table, *kept[1:])

    def kernel(*refs):
        distant, (out_ref, *near), (table_ref, sems) = refs[: len(far)], refs[len(far) : -2], refs[-2:]
        vector_ref, position_ref = near[:2]
        copies = [
            pltpu.make_async_copy(source, target, sems.at[index])
            for index, (source, target) in enumerate(zip(distant, (near[0], table_ref, *near[1:]), strict=True))
        ]
        for copy in copies:
            copy.start()
        for copy in copies[:3]:
            copy.wait()
        vector = vector_ref[...]
        high = vector.astype(bf16)
        low = (vector - high.astype(f32)).astype(bf16)
        stacked = jnp.concatenate([high, high, low], 0)
        columns = jnp.dot(table_ref[...], stacked, preferred_element_type=f32)
        x_pos = (position_ref[...] // sizes.grid).astype(f32)
        y_pos = (position_ref[...] % sizes.grid).astype(f32)
        row = lax.broadcasted_iota(jnp.int32, (8, sizes.sticks_local), 0)
        tail = jnp.where(row == 0, x_pos, jnp.where(row == 1, y_pos, 0.0)).astype(bf16)
        for group in range(sizes.groups):
            out_ref[group, 0:block, :] = columns[group * block : (group + 1) * block].astype(bf16)
            out_ref[group, block:, :] = tail
        for copy in copies[3:]:
            copy.wait()

    return call_on_chip(
        kernel,
        "spread_sticks",
        (),
        (((sizes.groups, block + 8, sizes.sticks_local), bf16), *[(array.shape, array.dtype) for array in kept]),
        far,
        [pltpu.VMEM(z_table.shape, z_table.dtype), pltpu.SemaphoreType.DMA((len(far),))],
    )


def turn(position, size):
    angle = (position - 0.5 * size) * (2.0 * math.pi / size)
    square = angle * angle
    cosine = jnp.zeros_like(angle)
    sine = jnp.zeros_like(angle)
    for order in range(7, -1, -1):
        sign = (-1.0) ** order
        cosine = cosine * square + sign / math.factorial(2 * order)
        sine = sine * square + sign / math.factorial(2 * order + 1)
    return -cosine, -sine * angle


def anchor_of(position, grid_size):
    spot = lax.broadcasted_iota(jnp.int32, (1, grid_size), 1).astype(f32)

    def total(values):
        return jnp.sum(jnp.sum(values, axis=0, keepdims=True), axis=1, keepdims=True)

    cosine, sine = turn(position, grid_size)
    spot_cosine, spot_sine = turn(spot, grid_size)
    score = total(cosine) * spot_cosine + total(sine) * spot_sine
    best = jnp.max(score, axis=1, keepdims=True)
    return jnp.min(jnp.where(score >= best, spot, float(grid_size)), axis=1, keepdims=True)


def cross(first, second, line):
    if line % lanes == 0:
        count = first.shape[1] // line
        return [
            jnp.concatenate([side[:, i * line : (i + 1) * line] for side in (first, second)], 1) for i in range(count)
        ]
    low = lax.broadcasted_iota(jnp.int32, (first.shape[0], lanes), 1) < line
    results = []
    for start in range(0, first.shape[1], lanes):
        one, two = first[:, start : start + lanes], second[:, start : start + lanes]
        results.append(jnp.where(low, one, pltpu.roll(two, line, 1)))
        results.append(jnp.where(low, pltpu.roll(one, line, 1), two))
    return results


def apply_planes(sizes, received, near, later, psi_res):
    grid, box, line, rows = sizes.grid, sizes.box, sizes.line, sizes.rows
    groups, local, sticks = sizes.groups, sizes.sticks_local, sizes.sticks
    low_count, high_count = sizes.low_count, sizes.high_count
    columns = low_count * line
    half = high_count * rows

    psi_bytes, other_bytes = (sum(array.nbytes for array in arrays) for arrays in ((psi_res,), (received, received, near)))
    fits = psi_bytes + other_bytes < 3200000

    def kernel(in_ref, yb_ref, *refs):
        *distant, out_ref = refs[:5]
        scratch = refs[5:]
        if fits:
            *distant, psi_far = refs[:5]
            out_ref, psi_ref, *scratch = refs[5:]
            psi_copy = pltpu.make_async_copy(psi_far, psi_ref, scratch[-1].at[4])
        *near_refs, left_ref, hot_ref, a_ref, b_ref, field_ref, sems = scratch
        xb_ref, pot_ref, xf_ref, yf_ref = near_refs
        tables = [
            pltpu.make_async_copy(distant[index], near_refs[index], sems.at[slot])
            for slot, index in enumerate((0, 2, 3))
        ]
        pot_copy = pltpu.make_async_copy(distant[1], pot_ref, sems.at[3])
        for copy in (tables[0], pot_copy, *tables[1:]):
            copy.start()
        if fits:
            psi_copy.start()

        def relative(row):
            position = jnp.concatenate([in_ref[g, 2 * rows : 2 * rows + 8, :].astype(f32)[row : row + 1] for g in range(groups)], 0)
            moved = position - anchor_of(position, grid) + float(box // 2)
            moved = jnp.where(moved < 0, moved + float(grid), moved)
            return jnp.where(moved >= float(grid), moved - float(grid), moved)

        x_rel, y_rel = relative(0), relative(1)
        x_high = jnp.floor(x_rel * (1.0 / low_count))
        column = (x_rel - x_high * low_count) * float(line) + y_rel
        step = lax.broadcasted_iota(jnp.int32, (16, local), 0).astype(f32).astype(bf16)
        highs = []
        for g in range(groups):
            where = slice(g * local, (g + 1) * local)
            column_here = jnp.broadcast_to(column[g : g + 1], (16, local)).astype(bf16)
            for start in range(0, columns, 16):
                hot_ref[start : start + 16, where] = jnp.where(
                    column_here == step + jnp.asarray(start, bf16), jnp.asarray(1, bf16), jnp.asarray(0, bf16)
                )
            highs.append(jnp.broadcast_to(x_high[g : g + 1], (rows, local)))
            high_here = highs[g].astype(bf16)
            for part in range(2):
                values = in_ref[g, part * rows : (part + 1) * rows, :]
                for high in range(high_count):
                    start = (part * high_count + high) * rows
                    left_ref[start : start + rows, where] = jnp.where(
                        high_here == jnp.asarray(high, bf16), values, jnp.asarray(0, bf16)
                    )

        placed = lax.dot_general(left_ref[...], hot_ref[...], (((1,), (1,)), ((), ())), preferred_element_type=f32)
        placed = jnp.concatenate(cross(placed[:half], placed[half:], line), 0).astype(bf16)
        lines = jnp.dot(jnp.concatenate([placed, placed], 1), yb_ref[...], preferred_element_type=f32)
        for part in range(2):
            a_ref[part] = lines[:, part * grid : (part + 1) * grid]

        tables[0].wait()
        for first in range(0, rows, 2):
            high, low = [], []
            for plane in (first, first + 1):
                lines = jnp.concatenate([a_ref[part, pl.ds(plane, box, stride=rows), :] for part in range(2)], 0)
                high.append(lines.astype(bf16))
                low.append((lines - high[-1].astype(f32)).astype(bf16))
            high, low = jnp.concatenate(high, 1), jnp.concatenate(low, 1)
            field_ref[first // 2] = jnp.dot(xb_ref[...], jnp.concatenate([high, high, low], 0), preferred_element_type=f32)
        for copy in (pot_copy, tables[1], tables[2]):
            copy.wait()
        for first in range(0, rows, 2):
            weight = jnp.concatenate([pot_ref[first], pot_ref[first + 1]], 1)
            field = (field_ref[first // 2] * jnp.concatenate([weight, weight], 0)).astype(bf16)
            back = jnp.dot(xf_ref[...], field, preferred_element_type=f32)
            back = back[: 2 * box] + back[2 * box :]
            for index in range(2):
                for part in range(2):
                    b_ref[part, pl.ds(first + index, box, stride=rows), :] = back[
                        part * box : (part + 1) * box, index * grid : (index + 1) * grid
                    ]

        lines = jnp.concatenate([b_ref[0], b_ref[1]], 1).astype(bf16)
        boxed = jnp.dot(lines, yf_ref[...], preferred_element_type=f32)
        boxed = boxed[:, : 2 * line] + boxed[:, 2 * line :]
        if line % lanes == 0:
            parts = [
                jnp.concatenate([boxed[low * half : (low + 1) * half, part * line : (part + 1) * line] for low in range(low_count)], 1)
                for part in range(2)
            ]
        else:
            pairs = [
                cross(boxed[low * half : (low + 1) * half], boxed[(low + 1) * half : (low + 2) * half], line)
                for low in range(0, low_count, 2)
            ]
            parts = [jnp.concatenate([pair[part] for pair in pairs], 1) for part in range(2)]
        boxed = jnp.concatenate(parts, 0).astype(bf16)
        for first in range(0, groups, 2):
            found = jnp.dot(boxed, hot_ref[:, first * local : (first + 2) * local], preferred_element_type=f32)
            for g in (first, first + 1):
                for part in range(2):
                    total = jnp.zeros((rows, local), f32)
                    for high in range(high_count):
                        start = (part * high_count + high) * rows
                        piece = found[start : start + rows, (g - first) * local : (g - first + 1) * local]
                        total = total + jnp.where(highs[g] == float(high), piece, 0.0)
                    out_ref[g, part * rows : (part + 1) * rows, :] = total.astype(bf16)
        if fits:
            psi_copy.wait()

    extra = (psi_res,) if fits else ()
    picked, *brought = call_on_chip(
        kernel,
        "apply_planes",
        (received, near),
        (((groups, 2 * rows, local), bf16), *[(array.shape, array.dtype) for array in extra]),
        (*later, *extra),
        (
            *[pltpu.VMEM(array.shape, array.dtype) for array in later],
            pltpu.VMEM((2 * half, sticks), bf16),
            pltpu.VMEM((columns, sticks), bf16),
            pltpu.VMEM((2, box * rows, grid), f32),
            pltpu.VMEM((2, box * rows, grid), f32),
            pltpu.VMEM((rows // 2, 2 * grid, 2 * grid), f32),
            pltpu.SemaphoreType.DMA((5,)),
        ),
    )
    return picked, brought[0] if fits else psi_res


def image_sticks(sizes, columns, vector, positions):
    depth, local, grid = sizes.depth, sizes.sticks_local, sizes.grid
    height = 2 * depth

    def kernel(table_ref, columns_ref, vector_ref, position_ref, image_ref, rounded_ref, sums_ref):
        product = jnp.dot(table_ref[...], columns_ref[...], preferred_element_type=f32)
        applied = product[:height] + product[height:]
        vector = vector_ref[...]
        x_freq = signed_freq(position_ref[...] // grid, grid)
        y_freq = signed_freq(position_ref[...] % grid, grid)
        row = lax.broadcasted_iota(jnp.int32, (height, local), 0)
        z_freq = jnp.where(row < depth, row, row - depth) - depth // 2
        kinetic = kinetic_unit * (z_freq * z_freq + (x_freq * x_freq + y_freq * y_freq)).astype(f32)
        image = kinetic * vector + applied
        image_ref[...] = image
        rounded_ref[0:height, :] = vector.astype(bf16)
        rounded_ref[height:, :] = image.astype(bf16)
        sums_ref[0:1, :] = jnp.sum(vector * image, axis=0, keepdims=True)
        sums_ref[1:2, :] = jnp.sum(vector * vector, axis=0, keepdims=True)

    return call_on_chip(
        kernel,
        "image_sticks",
        (jnp.asarray(z_forward_table(sizes)), columns, vector, positions),
        (((height, local), f32), ((2 * height, local), bf16), ((2, local), f32)),
    )


def share(product, sums, groups):
    count, width = product.shape
    half = width // 2
    height = round_up(count // 2 + 2, 8)

    def kernel(product_ref, sums_ref, out_ref, sorted_ref):
        source = lax.broadcasted_iota(jnp.int32, (width, width), 0)
        target = lax.broadcasted_iota(jnp.int32, (width, width), 1)
        table = jnp.where(target == source % 2 * half + source // 2, 1.0, 0.0)
        sorted_ref[...] = jnp.dot(product_ref[...], table, precision=highest, preferred_element_type=f32)
        real = sorted_ref[pl.ds(0, count // 2, stride=2), :]
        imag = sorted_ref[pl.ds(1, count // 2, stride=2), :]
        low = lax.broadcasted_iota(jnp.int32, real.shape, 1) < half
        joined = jnp.where(low, real, -real) + pltpu.roll(imag, half, 1)
        fill = jnp.zeros((height - count // 2 - 2, width), f32)
        partial = jnp.concatenate([joined, sums_ref[...], fill], 0)
        for group in range(groups):
            out_ref[group] = partial

    return call_on_chip(
        kernel, "share", (product, sums), (((groups, height, width), f32),), scratch=(pltpu.VMEM((count, width), f32),)
    )[0]


def finish(copies, image, vector, band, band_total, res_count):
    count, height, width = copies.shape

    def kernel(band_ref, copies_ref, image_ref, vector_ref, residual_ref, ham_ref, inter_ref, total_ref):
        total = copies_ref[0]
        for index in range(1, count):
            total = total + copies_ref[index]
        tail = jnp.sum(total[2 * band_total : 2 * band_total + 2], axis=1, keepdims=True)
        residual_ref[...] = image_ref[...] - (tail[0:1] / tail[1:2]) * vector_ref[...]
        total_ref[...] = total
        for column in range(band_total):
            source = column ^ band_ref[0]
            for index, out_ref in enumerate((inter_ref, ham_ref)):
                row = total_ref[pl.ds(source * 2 + index, 1), :]
                for part in range(2):
                    out_ref[part, column : column + 1, :] = row[:, part * res_count : (part + 1) * res_count]

    spec = pl.BlockSpec(memory_space=pltpu.VMEM)
    operands = (copies, image, vector)
    projection = jax.ShapeDtypeStruct((2, band_total, res_count), f32)
    return pl.pallas_call(
        kernel,
        out_shape=(jax.ShapeDtypeStruct(image.shape, f32), projection, projection),
        in_specs=[pl.BlockSpec(memory_space=pltpu.SMEM)] + [spec] * 3,
        out_specs=(spec,) * 3,
        scratch_shapes=[pltpu.VMEM((height, width), f32)],
        name="finish",
    )(band, *[pltpu.with_memory_space_constraint(operand, pltpu.VMEM) for operand in operands])


def shards(psi_res, correction, local_potential, stick_xy):
    groups, band_total = lax.axis_size("pw"), lax.axis_size("band")
    planes, grid_size = local_potential.shape[:2]
    _, _, stick_depth, sticks_local = correction.shape
    res_count = psi_res.shape[0]
    sizes = Sizes(groups, planes, grid_size, stick_depth, sticks_local)
    potential = jnp.pad(local_potential, ((0, sizes.rows - planes), (0, 0), (0, 0)))
    vector = correction.reshape(2 * stick_depth, sticks_local)

    y_back, x_back, x_forward, y_forward = [jnp.asarray(table) for table in plane_tables(sizes)]
    moving, vector, positions, y_back = spread_sticks(sizes, vector, stick_xy, y_back)
    later = (x_back, potential, x_forward, y_forward)
    moving = lax.all_to_all(moving, "pw", split_axis=0, concat_axis=0, tiled=True)
    picked, psi_near = apply_planes(sizes, moving, y_back, later, psi_res.reshape(2 * res_count, stick_depth, sticks_local))
    picked = lax.all_to_all(picked, "pw", split_axis=0, concat_axis=0, tiled=True)
    picked = picked.reshape(2 * sizes.rows * groups, sticks_local)
    image, rounded, sums = image_sticks(sizes, picked, vector, positions)

    blocks = [rounded] + [
        lax.ppermute(rounded, "band", [(i, i ^ step) for i in range(band_total)]) for step in range(1, band_total)
    ]
    joined = jnp.concatenate(blocks, 0).reshape(4 * band_total, stick_depth, sticks_local)
    product = lax.dot_general(
        joined,
        psi_near,
        (((1, 2), (1, 2)), ((), ())),
        preferred_element_type=f32,
    )
    band = lax.axis_index("band")[None]
    product, band = lax.optimization_barrier((product, band))
    copies = share(product, sums, groups)
    copies = lax.all_to_all(copies, "pw", split_axis=0, concat_axis=0, tiled=True)
    residual, hamiltonian, intersection = finish(copies, image, vector, band, band_total, res_count)
    return (
        residual.reshape(correction.shape),
        jnp.transpose(hamiltonian, (0, 2, 1)),
        jnp.transpose(intersection, (0, 2, 1)),
    )


def solution(mesh):
    return jax.shard_map(
        shards,
        mesh=mesh,
        in_specs=(
            P("band", None, None, "pw"),
            P("band", None, None, "pw"),
            P("pw", None, None),
            P("pw"),
        ),
        out_specs=(P("band", None, None, "pw"), P(None, "band", None), P(None, "band", None)),
        check_vma=False,
    )
```

```python
import math

import jax
import jax.numpy as jnp
import numpy as np
from jax import lax
from jax.experimental import pallas as pl
from jax.experimental.pallas import tpu as pltpu
from jax.sharding import PartitionSpec as P

kinetic_unit = 0.002
highest = lax.Precision.HIGHEST
lanes = 128
f32 = jnp.float32
bf16 = jnp.bfloat16


def round_up(count, step):
    return -(-count // step) * step


def signed_freq(index, grid_size):
    return jnp.where(index < grid_size // 2, index, index - grid_size)


def phases(out_index, in_index, direction, grid_size):
    angles = (out_index[:, None] * in_index[None, :]) % grid_size * (2.0 * math.pi / grid_size)
    cosine, sine = np.cos(angles), direction * np.sin(angles)
    return np.stack([np.stack([cosine, -sine], 1), np.stack([sine, cosine], 1)], 0)


def split(table, count):
    pot_copy = []
    rest = np.asarray(table, np.float64)
    for _ in range(count):
        piece = rest.astype(jnp.bfloat16)
        pot_copy.append(piece)
        rest = rest - piece.astype(np.float64)
    return pot_copy


class Sizes:
    def __init__(self, groups, planes, grid_size, stick_depth, sticks_local):
        self.groups, self.planes = groups, planes
        self.grid, self.depth, self.sticks_local = grid_size, stick_depth, sticks_local
        self.rows = round_up(planes, 16)
        self.sticks = groups * sticks_local
        self.box = round_up(2 * math.ceil(math.sqrt(self.sticks / math.pi)) + 2, 8)
        self.line = round_up(self.box, 64)
        self.low_count = max(1, 256 // self.line)
        self.high_count = self.box // self.low_count


def z_rows(sizes):
    group = np.repeat(np.arange(sizes.groups), sizes.rows)
    plane = np.tile(np.arange(sizes.rows), sizes.groups)
    return group * sizes.planes + plane, plane < sizes.planes


def z_back_table(sizes):
    z_freq = np.arange(sizes.depth) - sizes.depth // 2
    z_index, real = z_rows(sizes)
    table = phases(z_index, z_freq, 1, sizes.grid) * real[None, :, None, None]
    table = table.reshape(2, sizes.groups, sizes.rows, 2 * sizes.depth)
    high, low = split(table.transpose(1, 0, 2, 3).reshape(-1, 2 * sizes.depth), 2)
    return np.concatenate([high, low, high], 1)


def z_forward_table(sizes):
    z_freq = np.arange(sizes.depth) - sizes.depth // 2
    z_index, real = z_rows(sizes)
    table = phases(z_freq, z_index, -1, sizes.grid) * real / float(sizes.grid**3)
    table = table.reshape(2 * sizes.depth, 2, sizes.groups, sizes.rows)
    table = table.transpose(0, 2, 1, 3).reshape(2 * sizes.depth, -1)
    return np.concatenate(split(table, 2), 0)


def plane_tables(sizes):
    grid = np.arange(sizes.grid)
    y_freq = np.arange(sizes.line) - sizes.box // 2
    order = np.arange(sizes.box).reshape(sizes.high_count, sizes.low_count).T.reshape(-1)
    x_freq = order - sizes.box // 2
    inside = np.arange(sizes.line) < sizes.box
    y_back = phases(grid, y_freq, 1, sizes.grid) * inside
    y_back = y_back.reshape(2 * sizes.grid, -1).T
    y_forward = phases(y_freq, grid, -1, sizes.grid) * inside[None, :, None, None]
    y_forward = y_forward.reshape(-1, 2 * sizes.grid).T
    x_back = phases(grid, x_freq, 1, sizes.grid).reshape(2 * sizes.grid, -1)
    x_forward = phases(x_freq, grid, -1, sizes.grid).reshape(-1, 2 * sizes.grid)
    y_back = np.concatenate(split(y_back, 2), 0)
    x_high, x_low = split(x_back, 2)
    x_back = np.concatenate([x_high, x_low, x_high], 1)
    x_forward = np.concatenate(split(x_forward, 2), 0)
    y_forward = np.concatenate(split(y_forward, 2), 1)
    return y_back, x_back, x_forward, y_forward


def call_on_chip(kernel, name, operands, shapes, far=(), scratch=()):
    spec = pl.BlockSpec(memory_space=pltpu.VMEM)
    return pl.pallas_call(
        kernel,
        out_shape=tuple(pltpu.VMEM(shape, dtype) for shape, dtype in shapes),
        in_specs=[spec] * len(operands) + [pl.BlockSpec(memory_space=pl.ANY)] * len(far),
        out_specs=(spec,) * len(shapes),
        scratch_shapes=list(scratch),
        name=name,
    )(*[pltpu.with_memory_space_constraint(operand, pltpu.VMEM) for operand in operands], *far)


def spread_sticks(sizes, vector, positions, y_back):
    block = 2 * sizes.rows
    z_table = jnp.asarray(z_back_table(sizes))
    kept = (vector, positions[None, :], y_back)
    far = (kept[0], z_table, *kept[1:])

    def kernel(*refs):
        distant, (out_ref, *near), (table_ref, sems) = refs[: len(far)], refs[len(far) : -2], refs[-2:]
        vector_ref, position_ref = near[:2]
        copies = [
            pltpu.make_async_copy(source, target, sems.at[index])
            for index, (source, target) in enumerate(zip(distant, (near[0], table_ref, *near[1:]), strict=True))
        ]
        for copy in copies:
            copy.start()
        for copy in copies[:3]:
            copy.wait()
        vector = vector_ref[...]
        high = vector.astype(bf16)
        low = (vector - high.astype(f32)).astype(bf16)
        stacked = jnp.concatenate([high, high, low], 0)
        columns = jnp.dot(table_ref[...], stacked, preferred_element_type=f32)
        x_pos = (position_ref[...] // sizes.grid).astype(f32)
        y_pos = (position_ref[...] % sizes.grid).astype(f32)
        row = lax.broadcasted_iota(jnp.int32, (8, sizes.sticks_local), 0)
        tail = jnp.where(row == 0, x_pos, jnp.where(row == 1, y_pos, 0.0)).astype(bf16)
        for group in range(sizes.groups):
            out_ref[group, 0:block, :] = columns[group * block : (group + 1) * block].astype(bf16)
            out_ref[group, block:, :] = tail
        for copy in copies[3:]:
            copy.wait()

    return call_on_chip(
        kernel,
        "spread_sticks",
        (),
        (((sizes.groups, block + 8, sizes.sticks_local), bf16), *[(array.shape, array.dtype) for array in kept]),
        far,
        [pltpu.VMEM(z_table.shape, z_table.dtype), pltpu.SemaphoreType.DMA((len(far),))],
    )


def turn(position, size):
    angle = (position - 0.5 * size) * (2.0 * math.pi / size)
    square = angle * angle
    cosine = jnp.zeros_like(angle)
    sine = jnp.zeros_like(angle)
    for order in range(7, -1, -1):
        sign = (-1.0) ** order
        cosine = cosine * square + sign / math.factorial(2 * order)
        sine = sine * square + sign / math.factorial(2 * order + 1)
    return -cosine, -sine * angle


def anchor_of(position, grid_size):
    spot = lax.broadcasted_iota(jnp.int32, (1, grid_size), 1).astype(f32)

    def total(values):
        return jnp.sum(jnp.sum(values, axis=0, keepdims=True), axis=1, keepdims=True)

    cosine, sine = turn(position, grid_size)
    spot_cosine, spot_sine = turn(spot, grid_size)
    score = total(cosine) * spot_cosine + total(sine) * spot_sine
    best = jnp.max(score, axis=1, keepdims=True)
    return jnp.min(jnp.where(score >= best, spot, float(grid_size)), axis=1, keepdims=True)


def cross(first, second, line):
    if line % lanes == 0:
        count = first.shape[1] // line
        return [
            jnp.concatenate([side[:, i * line : (i + 1) * line] for side in (first, second)], 1) for i in range(count)
        ]
    low = lax.broadcasted_iota(jnp.int32, (first.shape[0], lanes), 1) < line
    results = []
    for start in range(0, first.shape[1], lanes):
        one, two = first[:, start : start + lanes], second[:, start : start + lanes]
        results.append(jnp.where(low, one, pltpu.roll(two, line, 1)))
        results.append(jnp.where(low, pltpu.roll(one, line, 1), two))
    return results


def apply_planes(sizes, received, near, later, psi_res):
    grid, box, line, rows = sizes.grid, sizes.box, sizes.line, sizes.rows
    groups, local, sticks = sizes.groups, sizes.sticks_local, sizes.sticks
    low_count, high_count = sizes.low_count, sizes.high_count
    columns = low_count * line
    half = high_count * rows

    bands = psi_res.shape[0]
    psi_bytes, other_bytes = (sum(array.nbytes for array in arrays) for arrays in ((psi_res,), (received, received, near)))
    fits = psi_bytes + other_bytes < 3200000

    def kernel(in_ref, yb_ref, *refs):
        *distant, out_ref = refs[:5]
        scratch = refs[5:]
        if fits:
            *distant, psi_far = refs[:5]
            out_ref, psi_ref, *scratch = refs[5:]
            psi_copies = [
                pltpu.make_async_copy(
                    psi_far.at[:, part], psi_ref.at[part * bands : (part + 1) * bands], scratch[-1].at[4 + part]
                )
                for part in range(2)
            ]
        *near_refs, left_ref, hot_ref, a_ref, b_ref, field_ref, sems = scratch
        xb_ref, pot_ref, xf_ref, yf_ref = near_refs
        tables = [
            pltpu.make_async_copy(distant[index], near_refs[index], sems.at[slot])
            for slot, index in enumerate((0, 2, 3))
        ]
        pot_copy = pltpu.make_async_copy(distant[1], pot_ref, sems.at[3])
        for copy in (tables[0], pot_copy, *tables[1:]):
            copy.start()
        if fits:
            for copy in psi_copies:
                copy.start()

        def relative(row):
            position = jnp.concatenate([in_ref[g, 2 * rows : 2 * rows + 8, :].astype(f32)[row : row + 1] for g in range(groups)], 0)
            moved = position - anchor_of(position, grid) + float(box // 2)
            moved = jnp.where(moved < 0, moved + float(grid), moved)
            return jnp.where(moved >= float(grid), moved - float(grid), moved)

        x_rel, y_rel = relative(0), relative(1)
        x_high = jnp.floor(x_rel * (1.0 / low_count))
        column = (x_rel - x_high * low_count) * float(line) + y_rel
        step = lax.broadcasted_iota(jnp.int32, (16, local), 0).astype(f32).astype(bf16)
        highs = []
        for g in range(groups):
            where = slice(g * local, (g + 1) * local)
            column_here = jnp.broadcast_to(column[g : g + 1], (16, local)).astype(bf16)
            for start in range(0, columns, 16):
                hot_ref[start : start + 16, where] = jnp.where(
                    column_here == step + jnp.asarray(start, bf16), jnp.asarray(1, bf16), jnp.asarray(0, bf16)
                )
            highs.append(jnp.broadcast_to(x_high[g : g + 1], (rows, local)))
            high_here = highs[g].astype(bf16)
            for part in range(2):
                values = in_ref[g, part * rows : (part + 1) * rows, :]
                for high in range(high_count):
                    start = (part * high_count + high) * rows
                    left_ref[start : start + rows, where] = jnp.where(
                        high_here == jnp.asarray(high, bf16), values, jnp.asarray(0, bf16)
                    )

        placed = lax.dot_general(left_ref[...], hot_ref[...], (((1,), (1,)), ((), ())), preferred_element_type=f32)
        placed = jnp.concatenate(cross(placed[:half], placed[half:], line), 0).astype(bf16)
        lines = jnp.dot(jnp.concatenate([placed, placed], 1), yb_ref[...], preferred_element_type=f32)
        for part in range(2):
            a_ref[part] = lines[:, part * grid : (part + 1) * grid]

        tables[0].wait()
        for first in range(0, rows, 2):
            high, low = [], []
            for plane in (first, first + 1):
                lines = jnp.concatenate([a_ref[part, pl.ds(plane, box, stride=rows), :] for part in range(2)], 0)
                high.append(lines.astype(bf16))
                low.append((lines - high[-1].astype(f32)).astype(bf16))
            high, low = jnp.concatenate(high, 1), jnp.concatenate(low, 1)
            field_ref[first // 2] = jnp.dot(xb_ref[...], jnp.concatenate([high, high, low], 0), preferred_element_type=f32)
        for copy in (pot_copy, tables[1], tables[2]):
            copy.wait()
        for first in range(0, rows, 2):
            weight = jnp.concatenate([pot_ref[first], pot_ref[first + 1]], 1)
            field = (field_ref[first // 2] * jnp.concatenate([weight, weight], 0)).astype(bf16)
            back = jnp.dot(xf_ref[...], field, preferred_element_type=f32)
            back = back[: 2 * box] + back[2 * box :]
            for index in range(2):
                for part in range(2):
                    b_ref[part, pl.ds(first + index, box, stride=rows), :] = back[
                        part * box : (part + 1) * box, index * grid : (index + 1) * grid
                    ]

        lines = jnp.concatenate([b_ref[0], b_ref[1]], 1).astype(bf16)
        boxed = jnp.dot(lines, yf_ref[...], preferred_element_type=f32)
        boxed = boxed[:, : 2 * line] + boxed[:, 2 * line :]
        if line % lanes == 0:
            parts = [
                jnp.concatenate([boxed[low * half : (low + 1) * half, part * line : (part + 1) * line] for low in range(low_count)], 1)
                for part in range(2)
            ]
        else:
            pairs = [
                cross(boxed[low * half : (low + 1) * half], boxed[(low + 1) * half : (low + 2) * half], line)
                for low in range(0, low_count, 2)
            ]
            parts = [jnp.concatenate([pair[part] for pair in pairs], 1) for part in range(2)]
        boxed = jnp.concatenate(parts, 0).astype(bf16)
        for first in range(0, groups, 2):
            found = jnp.dot(boxed, hot_ref[:, first * local : (first + 2) * local], preferred_element_type=f32)
            for g in (first, first + 1):
                for part in range(2):
                    total = jnp.zeros((rows, local), f32)
                    for high in range(high_count):
                        start = (part * high_count + high) * rows
                        piece = found[start : start + rows, (g - first) * local : (g - first + 1) * local]
                        total = total + jnp.where(highs[g] == float(high), piece, 0.0)
                    out_ref[g, part * rows : (part + 1) * rows, :] = total.astype(bf16)
        if fits:
            for copy in psi_copies:
                copy.wait()

    extra = (psi_res,) if fits else ()
    picked, *brought = call_on_chip(
        kernel,
        "apply_planes",
        (received, near),
        (((groups, 2 * rows, local), bf16), *[((2 * bands, *array.shape[2:]), array.dtype) for array in extra]),
        (*later, *extra),
        (
            *[pltpu.VMEM(array.shape, array.dtype) for array in later],
            pltpu.VMEM((2 * half, sticks), bf16),
            pltpu.VMEM((columns, sticks), bf16),
            pltpu.VMEM((2, box * rows, grid), f32),
            pltpu.VMEM((2, box * rows, grid), f32),
            pltpu.VMEM((rows // 2, 2 * grid, 2 * grid), f32),
            pltpu.SemaphoreType.DMA((6,)),
        ),
    )
    if fits:
        return picked, brought[0]
    return picked, jnp.transpose(psi_res, (1, 0, 2, 3)).reshape(2 * bands, *psi_res.shape[2:])


def image_sticks(sizes, columns, vector, positions):
    depth, local, grid = sizes.depth, sizes.sticks_local, sizes.grid
    height = 2 * depth

    def kernel(table_ref, columns_ref, vector_ref, position_ref, image_ref, rounded_ref, sums_ref):
        product = jnp.dot(table_ref[...], columns_ref[...], preferred_element_type=f32)
        applied = product[:height] + product[height:]
        vector = vector_ref[...]
        x_freq = signed_freq(position_ref[...] // grid, grid)
        y_freq = signed_freq(position_ref[...] % grid, grid)
        row = lax.broadcasted_iota(jnp.int32, (height, local), 0)
        z_freq = jnp.where(row < depth, row, row - depth) - depth // 2
        kinetic = kinetic_unit * (z_freq * z_freq + (x_freq * x_freq + y_freq * y_freq)).astype(f32)
        image = kinetic * vector + applied
        image_ref[...] = image
        rounded_ref[0:height, :] = vector.astype(bf16)
        rounded_ref[height:, :] = image.astype(bf16)
        sums_ref[0:1, :] = jnp.sum(vector * image, axis=0, keepdims=True)
        sums_ref[1:2, :] = jnp.sum(vector * vector, axis=0, keepdims=True)

    return call_on_chip(
        kernel,
        "image_sticks",
        (jnp.asarray(z_forward_table(sizes)), columns, vector, positions),
        (((height, local), f32), ((2 * height, local), bf16), ((2, local), f32)),
    )


def share(product, sums, groups):
    count, width = product.shape
    half = width // 2
    height = round_up(count // 2 + 2, 8)

    def kernel(product_ref, sums_ref, out_ref):
        real = product_ref[pl.ds(0, count // 2, stride=2), :]
        imag = product_ref[pl.ds(1, count // 2, stride=2), :]
        low = lax.broadcasted_iota(jnp.int32, real.shape, 1) < half
        joined = jnp.where(low, real, -real) + pltpu.roll(imag, half, 1)
        fill = jnp.zeros((height - count // 2 - 2, width), f32)
        partial = jnp.concatenate([joined, sums_ref[...], fill], 0)
        for group in range(groups):
            out_ref[group] = partial

    return call_on_chip(kernel, "share", (product, sums), (((groups, height, width), f32),))[0]


def finish(copies, image, vector, band, band_total, res_count):
    count, height, width = copies.shape

    def kernel(band_ref, copies_ref, image_ref, vector_ref, residual_ref, ham_ref, inter_ref, total_ref):
        total = copies_ref[0]
        for index in range(1, count):
            total = total + copies_ref[index]
        tail = jnp.sum(total[2 * band_total : 2 * band_total + 2], axis=1, keepdims=True)
        residual_ref[...] = image_ref[...] - (tail[0:1] / tail[1:2]) * vector_ref[...]
        total_ref[...] = total
        for column in range(band_total):
            source = column ^ band_ref[0]
            for index, out_ref in enumerate((inter_ref, ham_ref)):
                row = total_ref[pl.ds(source * 2 + index, 1), :]
                for part in range(2):
                    out_ref[part, column : column + 1, :] = row[:, part * res_count : (part + 1) * res_count]

    spec = pl.BlockSpec(memory_space=pltpu.VMEM)
    operands = (copies, image, vector)
    projection = jax.ShapeDtypeStruct((2, band_total, res_count), f32)
    return pl.pallas_call(
        kernel,
        out_shape=(jax.ShapeDtypeStruct(image.shape, f32), projection, projection),
        in_specs=[pl.BlockSpec(memory_space=pltpu.SMEM)] + [spec] * 3,
        out_specs=(spec,) * 3,
        scratch_shapes=[pltpu.VMEM((height, width), f32)],
        name="finish",
    )(band, *[pltpu.with_memory_space_constraint(operand, pltpu.VMEM) for operand in operands])


def shards(psi_res, correction, local_potential, stick_xy):
    groups, band_total = lax.axis_size("pw"), lax.axis_size("band")
    planes, grid_size = local_potential.shape[:2]
    _, _, stick_depth, sticks_local = correction.shape
    res_count = psi_res.shape[0]
    sizes = Sizes(groups, planes, grid_size, stick_depth, sticks_local)
    potential = jnp.pad(local_potential, ((0, sizes.rows - planes), (0, 0), (0, 0)))
    vector = correction.reshape(2 * stick_depth, sticks_local)

    y_back, x_back, x_forward, y_forward = [jnp.asarray(table) for table in plane_tables(sizes)]
    moving, vector, positions, y_back = spread_sticks(sizes, vector, stick_xy, y_back)
    later = (x_back, potential, x_forward, y_forward)
    moving = lax.all_to_all(moving, "pw", split_axis=0, concat_axis=0, tiled=True)
    picked, psi_near = apply_planes(sizes, moving, y_back, later, psi_res)
    picked = lax.all_to_all(picked, "pw", split_axis=0, concat_axis=0, tiled=True)
    picked = picked.reshape(2 * sizes.rows * groups, sticks_local)
    image, rounded, sums = image_sticks(sizes, picked, vector, positions)

    blocks = [rounded] + [
        lax.ppermute(rounded, "band", [(i, i ^ step) for i in range(band_total)]) for step in range(1, band_total)
    ]
    joined = jnp.concatenate(blocks, 0).reshape(4 * band_total, stick_depth, sticks_local)
    product = lax.dot_general(
        joined,
        psi_near,
        (((1, 2), (1, 2)), ((), ())),
        preferred_element_type=f32,
    )
    band = lax.axis_index("band")[None]
    product, band = lax.optimization_barrier((product, band))
    copies = share(product, sums, groups)
    copies = lax.all_to_all(copies, "pw", split_axis=0, concat_axis=0, tiled=True)
    residual, hamiltonian, intersection = finish(copies, image, vector, band, band_total, res_count)
    return (
        residual.reshape(correction.shape),
        jnp.transpose(hamiltonian, (0, 2, 1)),
        jnp.transpose(intersection, (0, 2, 1)),
    )


def solution(mesh):
    return jax.shard_map(
        shards,
        mesh=mesh,
        in_specs=(
            P("band", None, None, "pw"),
            P("band", None, None, "pw"),
            P("pw", None, None),
            P("pw"),
        ),
        out_specs=(P("band", None, None, "pw"), P(None, "band", None), P(None, "band", None)),
        check_vma=False,
    )
```

```python
import math

import jax
import jax.numpy as jnp
import numpy as np
from jax import lax
from jax.experimental import pallas as pl
from jax.experimental.pallas import tpu as pltpu
from jax.sharding import PartitionSpec as P

kinetic_unit = 0.002
highest = lax.Precision.HIGHEST
lanes = 128
f32 = jnp.float32
bf16 = jnp.bfloat16


def round_up(count, step):
    return -(-count // step) * step


def signed_freq(index, grid_size):
    return jnp.where(index < grid_size // 2, index, index - grid_size)


def phases(out_index, in_index, direction, grid_size):
    angles = (out_index[:, None] * in_index[None, :]) % grid_size * (2.0 * math.pi / grid_size)
    cosine, sine = np.cos(angles), direction * np.sin(angles)
    return np.stack([np.stack([cosine, -sine], 1), np.stack([sine, cosine], 1)], 0)


def split(table, count):
    pot_copy = []
    rest = np.asarray(table, np.float64)
    for _ in range(count):
        piece = rest.astype(jnp.bfloat16)
        pot_copy.append(piece)
        rest = rest - piece.astype(np.float64)
    return pot_copy


class Sizes:
    def __init__(self, groups, planes, grid_size, stick_depth, sticks_local):
        self.groups, self.planes = groups, planes
        self.grid, self.depth, self.sticks_local = grid_size, stick_depth, sticks_local
        self.rows = round_up(planes, 16)
        self.sticks = groups * sticks_local
        self.box = round_up(2 * math.ceil(math.sqrt(self.sticks / math.pi)) + 2, 8)
        self.line = round_up(self.box, 64)
        self.low_count = max(1, 256 // self.line)
        self.high_count = self.box // self.low_count


def z_rows(sizes):
    group = np.repeat(np.arange(sizes.groups), sizes.rows)
    plane = np.tile(np.arange(sizes.rows), sizes.groups)
    return group * sizes.planes + plane, plane < sizes.planes


def z_back_table(sizes):
    z_freq = np.arange(sizes.depth) - sizes.depth // 2
    z_index, real = z_rows(sizes)
    table = phases(z_index, z_freq, 1, sizes.grid) * real[None, :, None, None]
    table = table.reshape(2, sizes.groups, sizes.rows, 2 * sizes.depth)
    high, low = split(table.transpose(1, 0, 2, 3).reshape(-1, 2 * sizes.depth), 2)
    return np.concatenate([high, low, high], 1)


def z_forward_table(sizes):
    z_freq = np.arange(sizes.depth) - sizes.depth // 2
    z_index, real = z_rows(sizes)
    table = phases(z_freq, z_index, -1, sizes.grid) * real / float(sizes.grid**3)
    table = table.reshape(2 * sizes.depth, 2, sizes.groups, sizes.rows)
    table = table.transpose(0, 2, 1, 3).reshape(2 * sizes.depth, -1)
    return np.concatenate(split(table, 2), 0)


def plane_tables(sizes):
    grid = np.arange(sizes.grid)
    y_freq = np.arange(sizes.line) - sizes.box // 2
    order = np.arange(sizes.box).reshape(sizes.high_count, sizes.low_count).T.reshape(-1)
    x_freq = order - sizes.box // 2
    inside = np.arange(sizes.line) < sizes.box
    y_back = phases(grid, y_freq, 1, sizes.grid) * inside
    y_back = y_back.reshape(2 * sizes.grid, -1).T
    y_forward = phases(y_freq, grid, -1, sizes.grid) * inside[None, :, None, None]
    y_forward = y_forward.reshape(-1, 2 * sizes.grid).T
    x_back = phases(grid, x_freq, 1, sizes.grid).reshape(2 * sizes.grid, -1)
    x_forward = phases(x_freq, grid, -1, sizes.grid).reshape(-1, 2 * sizes.grid)
    y_back = np.concatenate(split(y_back, 2), 0)
    x_high, x_low = split(x_back, 2)
    x_back = np.concatenate([x_high, x_low, x_high], 1)
    x_forward = np.concatenate(split(x_forward, 2), 0)
    y_forward = np.concatenate(split(y_forward, 2), 1)
    return y_back, x_back, x_forward, y_forward


def call_on_chip(kernel, name, operands, shapes, far=(), scratch=()):
    spec = pl.BlockSpec(memory_space=pltpu.VMEM)
    return pl.pallas_call(
        kernel,
        out_shape=tuple(pltpu.VMEM(shape, dtype) for shape, dtype in shapes),
        in_specs=[spec] * len(operands) + [pl.BlockSpec(memory_space=pl.ANY)] * len(far),
        out_specs=(spec,) * len(shapes),
        scratch_shapes=list(scratch),
        name=name,
    )(*[pltpu.with_memory_space_constraint(operand, pltpu.VMEM) for operand in operands], *far)


def spread_sticks(sizes, vector, positions, y_back):
    block = 2 * sizes.rows
    z_table = jnp.asarray(z_back_table(sizes))
    kept = (vector, positions[None, :], y_back)
    far = (kept[0], z_table, *kept[1:])

    def kernel(*refs):
        distant, (out_ref, *near), (table_ref, sems) = refs[: len(far)], refs[len(far) : -2], refs[-2:]
        vector_ref, position_ref = near[:2]
        copies = [
            pltpu.make_async_copy(source, target, sems.at[index])
            for index, (source, target) in enumerate(zip(distant, (near[0], table_ref, *near[1:]), strict=True))
        ]
        for copy in copies:
            copy.start()
        for copy in copies[:3]:
            copy.wait()
        vector = vector_ref[...]
        high = vector.astype(bf16)
        low = (vector - high.astype(f32)).astype(bf16)
        stacked = jnp.concatenate([high, high, low], 0)
        columns = jnp.dot(table_ref[...], stacked, preferred_element_type=f32)
        x_pos = (position_ref[...] // sizes.grid).astype(f32)
        y_pos = (position_ref[...] % sizes.grid).astype(f32)
        row = lax.broadcasted_iota(jnp.int32, (8, sizes.sticks_local), 0)
        tail = jnp.where(row == 0, x_pos, jnp.where(row == 1, y_pos, 0.0)).astype(bf16)
        for group in range(sizes.groups):
            out_ref[group, 0:block, :] = columns[group * block : (group + 1) * block].astype(bf16)
            out_ref[group, block:, :] = tail
        for copy in copies[3:]:
            copy.wait()

    return call_on_chip(
        kernel,
        "spread_sticks",
        (),
        (((sizes.groups, block + 8, sizes.sticks_local), bf16), *[(array.shape, array.dtype) for array in kept]),
        far,
        [pltpu.VMEM(z_table.shape, z_table.dtype), pltpu.SemaphoreType.DMA((len(far),))],
    )


def turn(position, size):
    angle = (position - 0.5 * size) * (2.0 * math.pi / size)
    square = angle * angle
    cosine = jnp.zeros_like(angle)
    sine = jnp.zeros_like(angle)
    for order in range(7, -1, -1):
        sign = (-1.0) ** order
        cosine = cosine * square + sign / math.factorial(2 * order)
        sine = sine * square + sign / math.factorial(2 * order + 1)
    return -cosine, -sine * angle


def anchor_of(position, grid_size):
    spot = lax.broadcasted_iota(jnp.int32, (1, grid_size), 1).astype(f32)

    def total(values):
        return jnp.sum(jnp.sum(values, axis=0, keepdims=True), axis=1, keepdims=True)

    cosine, sine = turn(position, grid_size)
    spot_cosine, spot_sine = turn(spot, grid_size)
    score = total(cosine) * spot_cosine + total(sine) * spot_sine
    best = jnp.max(score, axis=1, keepdims=True)
    return jnp.min(jnp.where(score >= best, spot, float(grid_size)), axis=1, keepdims=True)


def cross(first, second, line):
    if line % lanes == 0:
        count = first.shape[1] // line
        return [
            jnp.concatenate([side[:, i * line : (i + 1) * line] for side in (first, second)], 1) for i in range(count)
        ]
    low = lax.broadcasted_iota(jnp.int32, (first.shape[0], lanes), 1) < line
    results = []
    for start in range(0, first.shape[1], lanes):
        one, two = first[:, start : start + lanes], second[:, start : start + lanes]
        results.append(jnp.where(low, one, pltpu.roll(two, line, 1)))
        results.append(jnp.where(low, pltpu.roll(one, line, 1), two))
    return results


def apply_planes(sizes, received, near, later, psi_res):
    grid, box, line, rows = sizes.grid, sizes.box, sizes.line, sizes.rows
    groups, local, sticks = sizes.groups, sizes.sticks_local, sizes.sticks
    low_count, high_count = sizes.low_count, sizes.high_count
    columns = low_count * line
    half = high_count * rows

    bands = psi_res.shape[0]
    psi_bytes, other_bytes = (sum(array.nbytes for array in arrays) for arrays in ((psi_res,), (received, received, near)))
    fits = psi_bytes + other_bytes < 3200000

    def kernel(in_ref, yb_ref, *refs):
        *distant, out_ref = refs[:5]
        scratch = refs[5:]
        if fits:
            *distant, psi_far = refs[:5]
            out_ref, psi_ref, *scratch = refs[5:]
            psi_copies = [
                pltpu.make_async_copy(
                    psi_far.at[:, part], psi_ref.at[part * bands : (part + 1) * bands], scratch[-1].at[4 + part]
                )
                for part in range(2)
            ]
        *near_refs, left_ref, hot_ref, a_ref, b_ref, field_ref, sems = scratch
        xb_ref, pot_ref, xf_ref, yf_ref = near_refs
        tables = [
            pltpu.make_async_copy(distant[index], near_refs[index], sems.at[slot])
            for slot, index in enumerate((0, 2, 3))
        ]
        pot_copy = pltpu.make_async_copy(distant[1], pot_ref, sems.at[3])
        for copy in (tables[0], pot_copy, *tables[1:]):
            copy.start()
        if fits:
            for copy in psi_copies:
                copy.start()

        def relative(row):
            position = jnp.concatenate([in_ref[g, 2 * rows : 2 * rows + 8, :].astype(f32)[row : row + 1] for g in range(groups)], 0)
            moved = position - anchor_of(position, grid) + float(box // 2)
            moved = jnp.where(moved < 0, moved + float(grid), moved)
            return jnp.where(moved >= float(grid), moved - float(grid), moved)

        x_rel, y_rel = relative(0), relative(1)
        x_high = jnp.floor(x_rel * (1.0 / low_count))
        column = (x_rel - x_high * low_count) * float(line) + y_rel
        step = lax.broadcasted_iota(jnp.int32, (16, local), 0).astype(f32).astype(bf16)
        highs = []
        for g in range(groups):
            where = slice(g * local, (g + 1) * local)
            column_here = jnp.broadcast_to(column[g : g + 1], (16, local)).astype(bf16)
            for start in range(0, columns, 16):
                hot_ref[start : start + 16, where] = jnp.where(
                    column_here == step + jnp.asarray(start, bf16), jnp.asarray(1, bf16), jnp.asarray(0, bf16)
                )
            highs.append(jnp.broadcast_to(x_high[g : g + 1], (rows, local)))
            high_here = highs[g].astype(bf16)
            for part in range(2):
                values = in_ref[g, part * rows : (part + 1) * rows, :]
                for high in range(high_count):
                    start = (part * high_count + high) * rows
                    left_ref[start : start + rows, where] = jnp.where(
                        high_here == jnp.asarray(high, bf16), values, jnp.asarray(0, bf16)
                    )

        placed = lax.dot_general(left_ref[...], hot_ref[...], (((1,), (1,)), ((), ())), preferred_element_type=f32)
        placed = jnp.concatenate(cross(placed[:half], placed[half:], line), 0).astype(bf16)
        lines = jnp.dot(jnp.concatenate([placed, placed], 1), yb_ref[...], preferred_element_type=f32)
        for part in range(2):
            a_ref[part] = lines[:, part * grid : (part + 1) * grid]

        tables[0].wait()
        for first in range(0, rows, 2):
            high, low = [], []
            for plane in (first, first + 1):
                lines = jnp.concatenate([a_ref[part, pl.ds(plane, box, stride=rows), :] for part in range(2)], 0)
                high.append(lines.astype(bf16))
                low.append((lines - high[-1].astype(f32)).astype(bf16))
            high, low = jnp.concatenate(high, 1), jnp.concatenate(low, 1)
            field_ref[first // 2] = jnp.dot(xb_ref[...], jnp.concatenate([high, high, low], 0), preferred_element_type=f32)
        for copy in (pot_copy, tables[1]):
            copy.wait()
        for first in range(0, rows, 2):
            weight = jnp.concatenate([pot_ref[first], pot_ref[first + 1]], 1)
            field = (field_ref[first // 2] * jnp.concatenate([weight, weight], 0)).astype(bf16)
            back = jnp.dot(xf_ref[...], field, preferred_element_type=f32)
            back = back[: 2 * box] + back[2 * box :]
            for index in range(2):
                for part in range(2):
                    b_ref[part, pl.ds(first + index, box, stride=rows), :] = back[
                        part * box : (part + 1) * box, index * grid : (index + 1) * grid
                    ]

        tables[2].wait()
        lines = jnp.concatenate([b_ref[0], b_ref[1]], 1).astype(bf16)
        boxed = jnp.dot(lines, yf_ref[...], preferred_element_type=f32)
        boxed = boxed[:, : 2 * line] + boxed[:, 2 * line :]
        if line % lanes == 0:
            parts = [
                jnp.concatenate([boxed[low * half : (low + 1) * half, part * line : (part + 1) * line] for low in range(low_count)], 1)
                for part in range(2)
            ]
        else:
            pairs = [
                cross(boxed[low * half : (low + 1) * half], boxed[(low + 1) * half : (low + 2) * half], line)
                for low in range(0, low_count, 2)
            ]
            parts = [jnp.concatenate([pair[part] for pair in pairs], 1) for part in range(2)]
        boxed = jnp.concatenate(parts, 0).astype(bf16)
        for first in range(0, groups, 2):
            found = jnp.dot(boxed, hot_ref[:, first * local : (first + 2) * local], preferred_element_type=f32)
            for g in (first, first + 1):
                for part in range(2):
                    total = jnp.zeros((rows, local), f32)
                    for high in range(high_count):
                        start = (part * high_count + high) * rows
                        piece = found[start : start + rows, (g - first) * local : (g - first + 1) * local]
                        total = total + jnp.where(highs[g] == float(high), piece, 0.0)
                    out_ref[g, part * rows : (part + 1) * rows, :] = total.astype(bf16)
        if fits:
            for copy in psi_copies:
                copy.wait()

    extra = (psi_res,) if fits else ()
    picked, *brought = call_on_chip(
        kernel,
        "apply_planes",
        (received, near),
        (((groups, 2 * rows, local), bf16), *[((2 * bands, *array.shape[2:]), array.dtype) for array in extra]),
        (*later, *extra),
        (
            *[pltpu.VMEM(array.shape, array.dtype) for array in later],
            pltpu.VMEM((2 * half, sticks), bf16),
            pltpu.VMEM((columns, sticks), bf16),
            pltpu.VMEM((2, box * rows, grid), f32),
            pltpu.VMEM((2, box * rows, grid), f32),
            pltpu.VMEM((rows // 2, 2 * grid, 2 * grid), f32),
            pltpu.SemaphoreType.DMA((6,)),
        ),
    )
    if fits:
        return picked, brought[0]
    return picked, jnp.transpose(psi_res, (1, 0, 2, 3)).reshape(2 * bands, *psi_res.shape[2:])


def image_sticks(sizes, columns, vector, positions):
    depth, local, grid = sizes.depth, sizes.sticks_local, sizes.grid
    height = 2 * depth

    def kernel(table_ref, columns_ref, vector_ref, position_ref, image_ref, rounded_ref, sums_ref):
        product = jnp.dot(table_ref[...], columns_ref[...], preferred_element_type=f32)
        applied = product[:height] + product[height:]
        vector = vector_ref[...]
        x_freq = signed_freq(position_ref[...] // grid, grid)
        y_freq = signed_freq(position_ref[...] % grid, grid)
        row = lax.broadcasted_iota(jnp.int32, (height, local), 0)
        z_freq = jnp.where(row < depth, row, row - depth) - depth // 2
        kinetic = kinetic_unit * (z_freq * z_freq + (x_freq * x_freq + y_freq * y_freq)).astype(f32)
        image = kinetic * vector + applied
        image_ref[...] = image
        rounded_ref[0:height, :] = vector.astype(bf16)
        rounded_ref[height:, :] = image.astype(bf16)
        sums_ref[0:1, :] = jnp.sum(vector * image, axis=0, keepdims=True)
        sums_ref[1:2, :] = jnp.sum(vector * vector, axis=0, keepdims=True)

    return call_on_chip(
        kernel,
        "image_sticks",
        (jnp.asarray(z_forward_table(sizes)), columns, vector, positions),
        (((height, local), f32), ((2 * height, local), bf16), ((2, local), f32)),
    )


def share(product, sums, groups):
    count, width = product.shape
    half = width // 2
    height = round_up(count // 2 + 2, 8)

    def kernel(product_ref, sums_ref, out_ref):
        real = product_ref[pl.ds(0, count // 2, stride=2), :]
        imag = product_ref[pl.ds(1, count // 2, stride=2), :]
        low = lax.broadcasted_iota(jnp.int32, real.shape, 1) < half
        joined = jnp.where(low, real, -real) + pltpu.roll(imag, half, 1)
        fill = jnp.zeros((height - count // 2 - 2, width), f32)
        partial = jnp.concatenate([joined, sums_ref[...], fill], 0)
        for group in range(groups):
            out_ref[group] = partial

    return call_on_chip(kernel, "share", (product, sums), (((groups, height, width), f32),))[0]


def finish(copies, image, vector, band, band_total, res_count):
    count, height, width = copies.shape

    def kernel(band_ref, copies_ref, image_ref, vector_ref, residual_ref, ham_ref, inter_ref, total_ref):
        total = copies_ref[0]
        for index in range(1, count):
            total = total + copies_ref[index]
        tail = jnp.sum(total[2 * band_total : 2 * band_total + 2], axis=1, keepdims=True)
        residual_ref[...] = image_ref[...] - (tail[0:1] / tail[1:2]) * vector_ref[...]
        total_ref[...] = total
        for column in range(band_total):
            source = column ^ band_ref[0]
            for index, out_ref in enumerate((inter_ref, ham_ref)):
                row = total_ref[pl.ds(source * 2 + index, 1), :]
                for part in range(2):
                    out_ref[part, column : column + 1, :] = row[:, part * res_count : (part + 1) * res_count]

    spec = pl.BlockSpec(memory_space=pltpu.VMEM)
    operands = (copies, image, vector)
    projection = jax.ShapeDtypeStruct((2, band_total, res_count), f32)
    return pl.pallas_call(
        kernel,
        out_shape=(jax.ShapeDtypeStruct(image.shape, f32), projection, projection),
        in_specs=[pl.BlockSpec(memory_space=pltpu.SMEM)] + [spec] * 3,
        out_specs=(spec,) * 3,
        scratch_shapes=[pltpu.VMEM((height, width), f32)],
        name="finish",
    )(band, *[pltpu.with_memory_space_constraint(operand, pltpu.VMEM) for operand in operands])


def shards(psi_res, correction, local_potential, stick_xy):
    groups, band_total = lax.axis_size("pw"), lax.axis_size("band")
    planes, grid_size = local_potential.shape[:2]
    _, _, stick_depth, sticks_local = correction.shape
    res_count = psi_res.shape[0]
    sizes = Sizes(groups, planes, grid_size, stick_depth, sticks_local)
    potential = jnp.pad(local_potential, ((0, sizes.rows - planes), (0, 0), (0, 0)))
    vector = correction.reshape(2 * stick_depth, sticks_local)

    y_back, x_back, x_forward, y_forward = [jnp.asarray(table) for table in plane_tables(sizes)]
    moving, vector, positions, y_back = spread_sticks(sizes, vector, stick_xy, y_back)
    later = (x_back, potential, x_forward, y_forward)
    moving = lax.all_to_all(moving, "pw", split_axis=0, concat_axis=0, tiled=True)
    picked, psi_near = apply_planes(sizes, moving, y_back, later, psi_res)
    picked = lax.all_to_all(picked, "pw", split_axis=0, concat_axis=0, tiled=True)
    picked = picked.reshape(2 * sizes.rows * groups, sticks_local)
    image, rounded, sums = image_sticks(sizes, picked, vector, positions)

    blocks = [rounded] + [
        lax.ppermute(rounded, "band", [(i, i ^ step) for i in range(band_total)]) for step in range(1, band_total)
    ]
    joined = jnp.concatenate(blocks, 0).reshape(4 * band_total, stick_depth, sticks_local)
    product = lax.dot_general(
        joined,
        psi_near,
        (((1, 2), (1, 2)), ((), ())),
        preferred_element_type=f32,
    )
    band = lax.axis_index("band")[None]
    product, band = lax.optimization_barrier((product, band))
    copies = share(product, sums, groups)
    copies = lax.all_to_all(copies, "pw", split_axis=0, concat_axis=0, tiled=True)
    residual, hamiltonian, intersection = finish(copies, image, vector, band, band_total, res_count)
    return (
        residual.reshape(correction.shape),
        jnp.transpose(hamiltonian, (0, 2, 1)),
        jnp.transpose(intersection, (0, 2, 1)),
    )


def solution(mesh):
    return jax.shard_map(
        shards,
        mesh=mesh,
        in_specs=(
            P("band", None, None, "pw"),
            P("band", None, None, "pw"),
            P("pw", None, None),
            P("pw"),
        ),
        out_specs=(P("band", None, None, "pw"), P(None, "band", None), P(None, "band", None)),
        check_vma=False,
    )
```
